256 devices in a mesh: cuts: 2 (over core), tile: 128 (over z, x, y).
Axes of the slice: x: 4, y: 4, z: 8, core: 2. Of those that a mesh axis runs over, the one named last changes fastest.
Arguments:
- object_slices: float32 [2, 2, 2048, 32768], P('cuts', None, None, 'tile'), may hold values from -5 to 5
- probe_field: float32 [2, 256, 256], replicated, may hold values from -4 to 4
- slice_phase: float32 [2, 256, 256], P('cuts'), may hold values from -3.140625 to 3.140625
- intensity: float32 [128, 8, 256, 256], P('tile'), may hold values from 0 to 1
- counts: int32 [128], P('tile'), may hold values from 1 to 6, as said below
- chosen: int32 [128, 6], P('tile'), may hold values from 0 to 7, as said below
- row_offset: int32 [128, 8], P('tile'), may hold values from 0 to 1792
- column_offset: int32 [128, 8], P('tile'), may hold values from 0 to 255
Outputs:
- object_grad: float32 [2, 2, 2048, 32768], P('cuts', None, None, 'tile')
The draws below stay inside these ranges and needn't reach their ends.
Inputs may be any that keep to these rules, and one draw needn't show every extreme that they name: `counts`: live slots of a tile; some tile has exactly 6. `chosen`: distinct within a tile.
All inputs are finite; a program needn't handle non-finite values.
Results may differ from the reference program's by a relative error of at most 0.039.
Values may be sent and summed in bfloat16 or wider, within the bound.
A program may use at most 128 MiB of HBM per device.

```python
import jax
import jax.numpy as jnp
from jax import lax

NP = 256
HO = 2048
TW = 256
SCAN = 8
P_DEV = 6
SLICES = 2
TILES = 128
WIDTH = 32768


def draw_counts(key, part):
    first_key, second_key, third_key = jax.random.split(key, 3)
    first_draw = jax.random.randint(first_key, (TILES,), 0, P_DEV)
    second_draw = jax.random.randint(second_key, (TILES,), 0, P_DEV)
    busiest = jax.random.randint(third_key, (), 0, TILES)
    drawn = 1 + jnp.minimum(first_draw, second_draw)
    return jnp.where(jnp.arange(TILES) == busiest, P_DEV, drawn).astype(jnp.int32)


def draw_chosen(key, part):
    tile_keys = jax.random.split(jax.random.fold_in(key, 11), TILES)

    def one_tile(tile_key):
        return jax.random.permutation(tile_key, SCAN)[:P_DEV]
    return jax.vmap(one_tile)(tile_keys).astype(jnp.int32)


def plant(values, rng, smallest, high):
    dims = values.shape
    place = [jax.random.randint(jax.random.fold_in(rng, axis), (), 0, dims[axis]) for axis in range(len(dims))]
    values = values.at[tuple(place)].set(smallest)
    longest = dims.index(max(dims))
    place[longest] = (place[longest] + 1) % dims[longest]
    return values.at[tuple(place)].set(high)


def shard_levels(own_key, dims, cuts, low, top_value):
    gain, own = 1.0, jax.random.fold_in(own_key, 6)
    for dim, shards_of in cuts:
        heights = jnp.exp(jax.random.uniform(jax.random.fold_in(own, dim), (shards_of,), jnp.float32, low / len(cuts), top_value / len(cuts)))
        gain = gain * jnp.repeat(heights, dims[dim] // shards_of).reshape([-1 if axis == dim else 1 for axis in range(len(dims))])
    return gain


def gaussian(stream_key, extent, scale, limit, cuts=(), kind=jnp.bfloat16):
    factor_of = shard_levels(stream_key, extent, cuts, -0.22, 0.18) if cuts else 1.0
    array = jax.random.normal(stream_key, extent, jnp.float32) * scale * factor_of
    return jnp.minimum(jnp.maximum(array, -limit), limit).astype(kind)


def setup_inputs(seed: int = 0) -> dict:
    key_list = jax.random.split(jax.random.key(seed), 9)
    object_slices = gaussian(key_list[0], (SLICES, 2, HO, WIDTH), 0.7, 5.0, ((0, 2), (3, 128)), jnp.float32)
    probe_field = gaussian(key_list[1], (2, NP, NP), 0.5, 4.0, (), jnp.float32)
    slice_phase = jnp.clip(jax.random.uniform(key_list[2], (SLICES, NP, NP), jnp.float32, -3.140625, 3.140625), -3.140625, 3.140625)
    intensity = jnp.clip(1.0 * jax.random.uniform(key_list[3], (TILES, SCAN, NP, NP), jnp.float32) ** shard_levels(key_list[3], (TILES, SCAN, NP, NP), ((0, 128),), -0.2, 0.2), 0.0, 1.0)
    counts = draw_counts(jax.random.fold_in(key_list[8], 71), 0)
    chosen = draw_chosen(jax.random.fold_in(key_list[8], 71), 0)
    row_offset = plant(jax.random.randint(key_list[6], (TILES, SCAN), 0, HO - NP + 1), jax.random.fold_in(key_list[6], 1), 0, HO - NP).astype(jnp.int32)
    column_offset = plant(jax.random.randint(key_list[7], (TILES, SCAN), 0, TW), jax.random.fold_in(key_list[7], 1), 0, TW - 1).astype(jnp.int32)
    return dict(object_slices=object_slices, probe_field=probe_field, slice_phase=slice_phase, intensity=intensity, counts=counts, chosen=chosen, row_offset=row_offset, column_offset=column_offset)


def rounded(values):
    return lax.optimization_barrier(values.astype(jnp.bfloat16)).astype(jnp.float32)


def make_table(length, direction):
    index = jnp.arange(length, dtype=jnp.int32)
    product = (index[:, None] * index[None, :]) % length
    angle = product.astype(jnp.float32) * (2.0 * jnp.pi / length)
    scale = length ** -0.5
    cosine = jnp.cos(angle) * scale
    sine = direction * jnp.sin(angle) * scale
    matrix = jnp.stack([jnp.stack([cosine, sine]), jnp.stack([-sine, cosine])])
    return matrix.astype(jnp.bfloat16).astype(jnp.float32)


def transform(field, matrix):
    halfway = jnp.einsum("cnm,cdmk->dnk", rounded(field), matrix, precision=lax.Precision.HIGHEST)
    return jnp.einsum("cdkn,cnm->dkm", matrix, rounded(halfway), precision=lax.Precision.HIGHEST)


def propagate(field, cosine, sine, forward_table, inverse_table):
    spectrum = transform(field, forward_table)
    turned = jnp.stack([spectrum[0] * cosine - spectrum[1] * sine, spectrum[0] * sine + spectrum[1] * cosine])
    return transform(turned, inverse_table)


def complex_mul(left, right):
    return jnp.stack([left[0] * right[0] - left[1] * right[1], left[0] * right[1] + left[1] * right[0]])


def conj_mul(left, right):
    return jnp.stack([left[0] * right[0] + left[1] * right[1], left[0] * right[1] - left[1] * right[0]])


def one_slot(patches, probe_field, cosines, sines, measured, is_live, forward_table, inverse_table):
    current = probe_field
    saved = []
    for slice_index in range(SLICES):
        saved.append(current)
        product = complex_mul(current, patches[slice_index])
        current = rounded(propagate(product, cosines[slice_index], sines[slice_index], forward_table, inverse_table))
    power = current[0] * current[0] + current[1] * current[1]
    cotangent = jnp.where(is_live, 2.0 * (power - measured) * current, 0.0)
    grads = [None] * SLICES
    for slice_index in reversed(range(SLICES)):
        spread = propagate(cotangent, cosines[slice_index], -sines[slice_index], forward_table, inverse_table)
        grads[slice_index] = conj_mul(saved[slice_index], spread)
        cotangent = conj_mul(patches[slice_index], spread)
    return jnp.stack(grads)


def reference(object_slices, probe_field, slice_phase, intensity, counts, chosen, row_offset, column_offset):
    cosines = jnp.cos(slice_phase)
    sines = jnp.sin(slice_phase)
    forward_table = make_table(NP, -1.0).astype(object_slices.dtype)
    inverse_table = make_table(NP, 1.0).astype(object_slices.dtype)
    margin = jnp.zeros((SLICES, 2, HO, TW), object_slices.dtype)
    padded = jnp.concatenate([object_slices, margin], axis=3)
    anchor = jnp.zeros((), jnp.int32)

    def tile_turn(carried, tile_index):
        start = (tile_index * TW).astype(jnp.int32)
        extended = lax.dynamic_slice(padded, (anchor, anchor, anchor, start), (SLICES, 2, HO, 2 * TW))
        canvas = jnp.zeros((SLICES, 2, HO, 2 * TW), object_slices.dtype)
        for slot_index in range(P_DEV):
            position = chosen[tile_index, slot_index].astype(jnp.int32)
            row_start = row_offset[tile_index, position].astype(jnp.int32)
            col_start = column_offset[tile_index, position].astype(jnp.int32)
            corner = (anchor, anchor, row_start, col_start)
            patches = lax.dynamic_slice(extended, corner, (SLICES, 2, NP, NP))
            is_live = slot_index < counts[tile_index]
            measured = intensity[tile_index, position]
            grads = one_slot(patches, probe_field, cosines, sines, measured, is_live, forward_table, inverse_table)
            current = lax.dynamic_slice(canvas, corner, (SLICES, 2, NP, NP))
            canvas = lax.dynamic_update_slice(canvas, current + grads, corner)
        return canvas[..., TW:], canvas[..., :TW] + carried

    initial = jnp.zeros((SLICES, 2, HO, TW), object_slices.dtype)
    _, pieces = lax.scan(tile_turn, initial, jnp.arange(TILES, dtype=jnp.int32))
    return jnp.moveaxis(pieces, 0, 3).reshape(SLICES, 2, HO, WIDTH)
```

```python
import jax
import jax.numpy as jnp
import numpy as np
from jax import lax
from jax.experimental import pallas as pl
from jax.experimental.pallas import tpu as pltpu
from jax.sharding import PartitionSpec as P

BF16 = jnp.bfloat16
F32 = jnp.float32


def dft_tables(length):
    index = np.arange(length, dtype=np.int32)
    product = index[:, None] * index[None, :] % length
    angle = product.astype(np.float32) * np.float32(2.0 * np.pi / length)
    scale = np.float32(length ** (-0.5))
    cosine = np.cos(angle) * scale
    sine = np.sin(angle) * scale
    forward = np.block([[cosine, -sine], [sine, cosine]])
    inverse = np.block([[cosine, sine], [-sine, cosine]])
    return forward.astype(BF16), inverse.astype(BF16)


def iota(shape, axis):
    return lax.broadcasted_iota(jnp.int32, shape, axis)


def slot_kernel(
    counts, chosen, row_offset, column_offset,
    obj_hbm, probe_hbm, phase_hbm, intensity_hbm, fwd_hbm, inv_hbm,
    index_out, own_out, halo_out,
    obj, probe, phase, trig, intensity, fwd, inv,
    own, own_send, halo, halo_send, terms, psi0, psi1, window, xbuf, ybuf,
    index_send, index_recv,
    in_sem, index_sem, phase_sem, own_ssem, own_rsem, halo_ssem, halo_rsem,
    out_sem, part_ssem, part_rsem, edge_ssem, edge_rsem,
):
    slots = chosen.shape[1]
    pairs = slots // 2
    size = probe.shape[-1]
    last_block = obj.shape[1] - 1
    core = lax.axis_index("cuts")
    tile = lax.axis_index("tile")
    tiles = lax.axis_size("tile")
    other = 1 - core
    right = lax.rem(tile + 1, tiles)
    left = lax.rem(tile + tiles - 1, tiles)

    loads = [
        pltpu.make_async_copy(obj_hbm, obj, in_sem.at[0]),
        pltpu.make_async_copy(phase_hbm, phase.at[core], in_sem.at[1]),
        pltpu.make_async_copy(probe_hbm, probe, in_sem.at[2]),
        pltpu.make_async_copy(fwd_hbm, fwd, in_sem.at[3]),
        pltpu.make_async_copy(inv_hbm, inv, in_sem.at[4]),
        pltpu.make_async_copy(intensity_hbm, intensity, in_sem.at[5]),
    ]
    for load in loads:
        load.start()

    barrier = pltpu.get_barrier_semaphore()
    peers = [{"cuts": other, "tile": tile}]
    for there in (left, right):
        for cut in (0, 1):
            peers.append({"cuts": cut, "tile": there})
    for peer in peers:
        pl.semaphore_signal(barrier, inc=1, device_id=peer)
    for j in range(slots):
        q = chosen[0, j]
        index_send[j] = row_offset[0, q]
        index_send[8 + j] = column_offset[0, q]
        index_send[16 + j] = (j < counts[0]).astype(jnp.int32)
    for j in list(range(slots, 8)) + list(range(8 + slots, 16)) + list(range(16 + slots, 32)):
        index_send[j] = 0
    pl.semaphore_wait(barrier, len(peers))

    index_copy = pltpu.make_async_remote_copy(
        index_send, index_recv, index_sem.at[0], index_sem.at[1],
        device_id={"cuts": core, "tile": right},
    )
    index_copy.start()
    loads[1].wait()
    phase_copy = pltpu.make_async_remote_copy(
        phase.at[core], phase.at[core], phase_sem.at[0], phase_sem.at[1],
        device_id={"cuts": other, "tile": tile},
    )
    phase_copy.start()
    loads[0].wait()
    index_copy.wait_recv()

    rows = iota((size, size), 0)
    lanes = iota((size, size), 1)

    def fold(row, plane):
        block = lax.shift_right_logical(row, 8)
        after = jnp.minimum(block + 1, last_block)
        here = obj[plane, block]
        below = obj[plane, after]
        return jnp.where(rows >= jnp.bitwise_and(row, size - 1), here, below).astype(BF16)

    def halo_copy(i, half):
        j = 2 * i + half
        return pltpu.make_async_remote_copy(
            halo_send.at[j], halo.at[i, core], halo_ssem.at[j], halo_rsem.at[i, core],
            device_id={"cuts": half, "tile": left},
        )

    def own_copy(i):
        return pltpu.make_async_remote_copy(
            own_send.at[i], own.at[i, core], own_ssem.at[i], own_rsem.at[i],
            device_id={"cuts": other, "tile": tile},
        )

    @pl.loop(0, pairs)
    def _(i):
        for half in (0, 1):
            row = index_recv[2 * i + half]
            for plane in (0, 1):
                halo_send[2 * i + half, plane] = fold(row, plane)
            halo_copy(i, half).start()

    @pl.loop(0, pairs)
    def _(i):
        row = index_send[2 * i + other]
        for plane in (0, 1):
            own_send[i, plane] = fold(row, plane)
        own_copy(i).start()
        row = index_send[2 * i + core]
        for plane in (0, 1):
            own[i, core, plane] = fold(row, plane)

    for k in range(32):
        index_out[k] = index_send[k]
        index_out[32 + k] = index_recv[k]

    phase_copy.wait_recv()

    @pl.loop(0, 2 * size // 32)
    def _(k):
        cut = k // (size // 32)
        start = pl.multiple_of(lax.rem(k, size // 32) * 32, 32)
        angle = phase[cut, pl.ds(start, 32), :]
        trig[cut, 0, pl.ds(start, 32), :] = jnp.cos(angle)
        trig[cut, 1, pl.ds(start, 32), :] = jnp.sin(angle)

    for load in loads[2:]:
        load.wait()

    def stage(real, imag):
        xbuf[:, :size] = real.astype(BF16)
        xbuf[:, size:] = imag.astype(BF16)

    def transform(right_table, left_table):
        halfway = jnp.dot(xbuf[...], right_table[...], preferred_element_type=F32)
        ybuf[:size, :] = halfway[:, :size].astype(BF16)
        ybuf[size:, :] = halfway[:, size:].astype(BF16)
        field = jnp.dot(left_table[...], ybuf[...], preferred_element_type=F32)
        return field[:size], field[size:]

    def propagate(real, imag, cut, sign):
        stage(real, imag)
        real, imag = transform(fwd, inv)
        cosine = trig[cut, 0]
        sine = trig[cut, 1] * sign
        stage(real * cosine - imag * sine, real * sine + imag * cosine)
        return transform(inv, fwd)

    def edge_copy(i, cut):
        j = 2 * i + core
        return pltpu.make_async_remote_copy(
            terms.at[i, cut], halo_out.at[j], edge_ssem.at[i, cut], edge_rsem.at[j],
            device_id={"cuts": cut, "tile": right},
        )

    def part_copy(i):
        j = 2 * i + core
        return pltpu.make_async_remote_copy(
            terms.at[i, other], own_out.at[j], part_ssem.at[i], part_rsem.at[i],
            device_id={"cuts": other, "tile": tile},
        )

    def keep_copy(i):
        return pltpu.make_async_copy(terms.at[i, core], own_out.at[2 * i + core], out_sem.at[i])

    @pl.loop(0, pairs)
    def _(i):
        j = 2 * i + core
        position = chosen[0, j]
        row = jnp.bitwise_and(row_offset[0, position], size - 1)
        column = column_offset[0, position]

        to_row = (rows == jnp.bitwise_and(lanes + row, size - 1)).astype(F32).astype(BF16)
        to_lane = (lanes == jnp.bitwise_and(rows + column, size - 1)).astype(F32).astype(BF16)

        def moved(value):
            moving = jnp.dot(value, to_lane, preferred_element_type=F32).astype(BF16)
            return jnp.dot(to_row, moving, preferred_element_type=F32)

        def shifted(value):
            high = value.astype(BF16)
            low = (value - high.astype(F32)).astype(BF16)
            return moved(high) + moved(low)

        for plane in (0, 1):
            psi0[plane] = shifted(probe[plane])
        own_copy(i).wait_recv()
        inside = lanes >= column
        scale = (tile < tiles - 1).astype(F32)
        for cut in (0, 1):
            pltpu.make_async_remote_copy(
                halo_send.at[0], halo.at[i, cut], halo_ssem.at[0], halo_rsem.at[i, cut],
                device_id={"cuts": cut, "tile": right},
            ).wait_recv()
            for plane in (0, 1):
                window[cut, plane] = jnp.where(
                    inside, own[i, cut, plane].astype(F32), halo[i, cut, plane].astype(F32) * scale
                )

        real, imag = psi0[0], psi0[1]
        o_real, o_imag = window[0, 0], window[0, 1]
        real, imag = propagate(real * o_real - imag * o_imag, real * o_imag + imag * o_real, 0, 1.0)
        psi1[0] = real.astype(BF16)
        psi1[1] = imag.astype(BF16)
        real, imag = psi1[0].astype(F32), psi1[1].astype(F32)
        o_real, o_imag = window[1, 0], window[1, 1]
        real, imag = propagate(real * o_real - imag * o_imag, real * o_imag + imag * o_real, 1, 1.0)
        real, imag = real.astype(BF16).astype(F32), imag.astype(BF16).astype(F32)
        factor = 2.0 * (real * real + imag * imag - shifted(intensity[position]))
        live = j < counts[0]
        real = jnp.where(live, factor * real, 0.0)
        imag = jnp.where(live, factor * imag, 0.0)

        real, imag = propagate(real, imag, 1, -1.0)
        w_real, w_imag = psi1[0].astype(F32), psi1[1].astype(F32)
        terms[i, 1, 0] = (w_real * real + w_imag * imag).astype(BF16)
        terms[i, 1, 1] = (w_real * imag - w_imag * real).astype(BF16)
        edge_copy(i, 1).start()
        o_real, o_imag = window[1, 0], window[1, 1]
        real, imag = propagate(
            o_real * real + o_imag * imag, o_real * imag - o_imag * real, 0, -1.0
        )
        w_real, w_imag = psi0[0], psi0[1]
        terms[i, 0, 0] = (w_real * real + w_imag * imag).astype(BF16)
        terms[i, 0, 1] = (w_real * imag - w_imag * real).astype(BF16)
        edge_copy(i, 0).start()
        part_copy(i).start()
        keep_copy(i).start()

    index_copy.wait_send()
    phase_copy.wait_send()

    @pl.loop(0, pairs)
    def _(i):
        own_copy(i).wait_send()
        part_copy(i).wait_send()
        part_copy(i).wait_recv()
        keep_copy(i).wait()
        for half in (0, 1):
            halo_copy(i, half).wait_send()
            edge_copy(i, half).wait_send()
            pltpu.make_async_remote_copy(
                terms.at[0, 0], halo_out.at[2 * i + half], edge_ssem.at[0, 0], edge_rsem.at[2 * i + half],
                device_id={"cuts": core, "tile": right},
            ).wait_recv()


def deposit_kernel(index, own_ref, halo_ref, out_ref):
    block = pl.program_id(0)
    slots = own_ref.shape[0]
    size = out_ref.shape[-1]
    rows = iota((size, size), 0)
    lanes = iota((size, size), 1)
    has_left = lax.axis_index("tile") > 0
    out_ref[...] = jnp.zeros_like(out_ref)

    for base, ref in ((0, own_ref), (32, halo_ref)):

        @pl.loop(0, slots)
        def _(j, base=base, ref=ref):
            row = index[base + j]
            column = index[base + 8 + j]
            first = lax.shift_right_logical(row, 8)
            start = jnp.bitwise_and(row, size - 1)
            live = index[base + 16 + j] > 0
            if base:
                live = live & has_left

            @pl.when(live & ((first == block) | (first + 1 == block)))
            def _():
                above = first == block
                low = jnp.where(above, start, 0)
                high = jnp.where(above, size, start)
                mask = (rows >= low) & (rows < high)
                mask = mask & ((lanes < column) if base else (lanes >= column))
                for plane in (0, 1):
                    out_ref[plane] += jnp.where(mask, ref[j, plane].astype(F32), 0.0)


def on_device(
    object_slices, probe_field, slice_phase, intensity, counts, chosen, row_offset, column_offset
):
    _, _, height, breadth = object_slices.shape
    size = probe_field.shape[-1]
    scan = row_offset.shape[1]
    slots = chosen.shape[1]
    pairs = slots // 2
    forward, inverse = dft_tables(size)
    smem = pl.BlockSpec(memory_space=pltpu.SMEM)
    anywhere = pl.BlockSpec(memory_space=pl.ANY)
    plane = (size, size)
    terms_shape = jax.ShapeDtypeStruct((slots, 2) + plane, BF16)
    dma = pltpu.SemaphoreType.DMA
    index, own, halo = pl.pallas_call(
        slot_kernel,
        out_shape=(jax.ShapeDtypeStruct((64,), jnp.int32), terms_shape, terms_shape),
        in_specs=[smem] * 4 + [anywhere] * 6,
        out_specs=(smem, anywhere, anywhere),
        scratch_shapes=[
            pltpu.VMEM((2, height // size) + plane, F32),
            pltpu.VMEM((2,) + plane, F32),
            pltpu.VMEM((2,) + plane, F32),
            pltpu.VMEM((2, 2) + plane, F32),
            pltpu.VMEM((scan,) + plane, F32),
            pltpu.VMEM((2 * size, 2 * size), BF16),
            pltpu.VMEM((2 * size, 2 * size), BF16),
            pltpu.VMEM((pairs, 2, 2) + plane, BF16),
            pltpu.VMEM((pairs, 2) + plane, BF16),
            pltpu.VMEM((pairs, 2, 2) + plane, BF16),
            pltpu.VMEM((slots, 2) + plane, BF16),
            pltpu.VMEM((pairs, 2, 2) + plane, BF16),
            pltpu.VMEM((2,) + plane, F32),
            pltpu.VMEM((2,) + plane, BF16),
            pltpu.VMEM((2, 2) + plane, F32),
            pltpu.VMEM((size, 2 * size), BF16),
            pltpu.VMEM((2 * size, size), BF16),
            pltpu.SMEM((32,), jnp.int32),
            pltpu.SMEM((32,), jnp.int32),
            dma((6,)),
            dma((2,)),
            dma((2,)),
            dma((pairs,)),
            dma((pairs,)),
            dma((slots,)),
            dma((pairs, 2)),
            dma((pairs,)),
            dma((pairs,)),
            dma((pairs,)),
            dma((pairs, 2)),
            dma((slots,)),
        ],
        compiler_params=pltpu.CompilerParams(
            collective_id=0, has_side_effects=True, vmem_limit_bytes=48 * 1024 * 1024
        ),
        name="slots",
    )(
        counts, chosen, row_offset, column_offset,
        object_slices.reshape(2, height // size, size, breadth), probe_field, slice_phase[0], intensity[0],
        jnp.asarray(forward), jnp.asarray(inverse),
    )
    resident = pl.BlockSpec(
        (slots, 2) + plane, lambda b, *_: (0, 0, 0, 0), pipeline_mode=pl.Buffered(1)
    )
    gradient = pl.pallas_call(
        deposit_kernel,
        grid_spec=pltpu.PrefetchScalarGridSpec(
            num_scalar_prefetch=1,
            grid=(height // size,),
            in_specs=[resident, resident],
            out_specs=pl.BlockSpec((2, size, breadth), lambda b, *_: (0, b, 0)),
        ),
        out_shape=jax.ShapeDtypeStruct((2, height, breadth), F32),
        compiler_params=pltpu.CompilerParams(vmem_limit_bytes=32 * 1024 * 1024),
        name="deposit",
    )(index, own, halo)
    return gradient[None]


def solution(mesh):
    return jax.shard_map(
        on_device,
        mesh=mesh,
        in_specs=(
            P("cuts", None, None, "tile"),
            P(),
            P("cuts", None, None),
            P("tile", None, None, None),
            P("tile"),
            P("tile", None),
            P("tile", None),
            P("tile", None),
        ),
        out_specs=P("cuts", None, None, "tile"),
        check_vma=False,
    )
```

```python
import jax
import jax.numpy as jnp
import numpy as np
from jax import lax
from jax.experimental import pallas as pl
from jax.experimental.pallas import tpu as pltpu
from jax.sharding import PartitionSpec as P

BF16 = jnp.bfloat16
F32 = jnp.float32


def dft_tables(length):
    index = np.arange(length, dtype=np.int32)
    product = index[:, None] * index[None, :] % length
    angle = product.astype(np.float32) * np.float32(2.0 * np.pi / length)
    scale = np.float32(length ** (-0.5))
    cosine = np.cos(angle) * scale
    sine = np.sin(angle) * scale
    forward = np.block([[cosine, -sine], [sine, cosine]])
    inverse = np.block([[cosine, sine], [-sine, cosine]])
    return forward.astype(BF16), inverse.astype(BF16)


def iota(shape, axis):
    return lax.broadcasted_iota(jnp.int32, shape, axis)


def slot_of(item, cut):
    return 2 * jnp.where(item == 0, 0, jnp.where(item == 2, 1, 2)) + cut


def slot_kernel(
    counts_hbm, chosen_hbm, row_hbm, column_hbm,
    obj_hbm, probe_hbm, phase_hbm, intensity_hbm, fwd_hbm, inv_hbm,
    index_out, out,
    obj, probe, phase, trig, intensity, fwd, inv,
    own, own_send, far, send_left, send_right, level_send, level_far, measured,
    terms, psi0, psi1, window, xbuf, ybuf,
    index, counts, chosen, row_offset, column_offset,
    in_sem, index_sem, phase_sem, level_sem, own_ssem, own_rsem, left_ssem, right_ssem, far_rsem,
    keep_sem, part_ssem, part_rsem, edge_ssem, edge_rsem,
):
    slots = chosen.shape[1]
    size = probe.shape[-1]
    items = terms.shape[0]
    last_block = obj.shape[1] - 1
    core = lax.axis_index("cuts")
    tile = lax.axis_index("tile")
    tiles = lax.axis_size("tile")
    other = 1 - core
    right = lax.rem(tile + 1, tiles)
    left = lax.rem(tile + tiles - 1, tiles)
    has_left = tile > 0
    has_right = tile < tiles - 1
    partner = {"cuts": other, "tile": tile}

    def copy_in(source, target, number):
        return pltpu.make_async_copy(source, target, in_sem.at[number])

    scalars = [
        copy_in(counts_hbm, counts, 0),
        copy_in(chosen_hbm, chosen, 1),
        copy_in(row_hbm, row_offset, 2),
        copy_in(column_hbm, column_offset, 3),
    ]
    load_obj = copy_in(obj_hbm, obj, 4)
    load_phase = copy_in(phase_hbm, phase.at[core], 5)
    load_intensity = copy_in(intensity_hbm, intensity, 6)
    rest = [copy_in(probe_hbm, probe, 7), copy_in(fwd_hbm, fwd, 8), copy_in(inv_hbm, inv, 9)]
    for load in scalars + [load_obj, load_phase, load_intensity] + rest:
        load.start()

    for k in range(32):
        index[0, k] = 0

    @pl.when(tile == 0)
    def _():
        for k in range(32):
            index[1, k] = 0

    barrier = pltpu.get_barrier_semaphore()
    pl.semaphore_signal(barrier, inc=1, device_id=partner)
    for there, reached in ((left, has_left), (right, has_right)):

        @pl.when(reached)
        def _(there=there):
            for cut in (0, 1):
                pl.semaphore_signal(barrier, inc=1, device_id={"cuts": cut, "tile": there})

    for load in scalars:
        load.wait()
    for j in range(slots):
        q = chosen[0, j]
        index[0, j] = row_offset[0, q]
        index[0, 8 + j] = column_offset[0, q]
        index[0, 16 + j] = (j < counts[0]).astype(jnp.int32)

    rows = iota((size, size), 0)
    lanes = iota((size, size), 1)

    def fold(row, plane):
        block = lax.shift_right_logical(row, 8)
        after = jnp.minimum(block + 1, last_block)
        here = obj[plane, block]
        below = obj[plane, after]
        return jnp.where(rows >= jnp.bitwise_and(row, size - 1), here, below).astype(BF16)

    index_copy = pltpu.make_async_remote_copy(
        index.at[0], index.at[1], index_sem.at[0], index_sem.at[1],
        device_id={"cuts": core, "tile": right},
    )
    phase_copy = pltpu.make_async_remote_copy(
        phase.at[core], phase.at[core], phase_sem.at[0], phase_sem.at[1], device_id=partner
    )
    level_copy = pltpu.make_async_remote_copy(
        level_send, level_far, level_sem.at[0], level_sem.at[1],
        device_id={"cuts": core, "tile": right},
    )

    def right_copy(half):
        return pltpu.make_async_remote_copy(
            send_right.at[half], far.at[1, core], right_ssem.at[half], far_rsem.at[1, core],
            device_id={"cuts": half, "tile": right},
        )

    def left_copy(j):
        item = 2 * (j // 2)
        return pltpu.make_async_remote_copy(
            send_left.at[j], far.at[item, core], left_ssem.at[j], far_rsem.at[item, core],
            device_id={"cuts": j % 2, "tile": left},
        )

    def own_copy(item):
        return pltpu.make_async_remote_copy(
            own_send.at[item], own.at[item, core], own_ssem.at[item], own_rsem.at[item],
            device_id=partner,
        )

    def near_windows(item):
        flip = int(item == 1)
        row = index[flip, slot_of(item, other)]
        for plane in (0, 1):
            own_send[item, plane] = fold(row, plane)
        own_copy(item).start()
        row = index[flip, slot_of(item, core)]
        for plane in (0, 1):
            own[item, core, plane] = fold(row, plane)

    load_obj.wait()
    for half in (0, 1):
        for plane in (0, 1):
            send_right[half, plane] = fold(index[0, slots - 2 + half], plane)

    peers = 1 + 2 * has_left.astype(jnp.int32) + 2 * has_right.astype(jnp.int32)
    pl.semaphore_wait(barrier, peers)

    @pl.when(has_right)
    def _():
        index_copy.start()
        right_copy(0).start()
        right_copy(1).start()

    load_phase.wait()
    phase_copy.start()
    near_windows(0)

    @pl.when(has_left)
    def _():
        index_copy.wait_recv()
        for j in range(slots - 2):
            for plane in (0, 1):
                send_left[j, plane] = fold(index[1, j], plane)
            left_copy(j).start()

    load_intensity.wait()

    @pl.when(has_right)
    def _():
        level_send[...] = intensity[chosen[0, slots - 2 + core]].astype(BF16)
        level_copy.start()

    near_windows(2)

    @pl.when(has_left)
    def _():
        near_windows(1)

    @pl.when(jnp.logical_not(has_right))
    def _():
        near_windows(3)

    for k in range(32):
        index_out[k] = index[0, k]
        index_out[32 + k] = index[1, k]

    phase_copy.wait_recv()

    @pl.loop(0, 2 * size // 32)
    def _(k):
        cut = k // (size // 32)
        start = pl.multiple_of(lax.rem(k, size // 32) * 32, 32)
        angle = phase[cut, pl.ds(start, 32), :]
        trig[cut, 0, pl.ds(start, 32), :] = jnp.cos(angle)
        trig[cut, 1, pl.ds(start, 32), :] = jnp.sin(angle)

    for load in rest:
        load.wait()

    def stage(real, imag):
        xbuf[:, :size] = real.astype(BF16)
        xbuf[:, size:] = imag.astype(BF16)

    def transform(right_table, left_table):
        halfway = jnp.dot(xbuf[...], right_table[...], preferred_element_type=F32)
        ybuf[:size, :] = halfway[:, :size].astype(BF16)
        ybuf[size:, :] = halfway[:, size:].astype(BF16)
        field = jnp.dot(left_table[...], ybuf[...], preferred_element_type=F32)
        return field[:size], field[size:]

    def propagate(real, imag, cut, sign):
        stage(real, imag)
        real, imag = transform(fwd, inv)
        cosine = trig[cut, 0]
        sine = trig[cut, 1] * sign
        stage(real * cosine - imag * sine, real * sine + imag * cosine)
        return transform(inv, fwd)

    def kind(item):
        return (item == 1).astype(jnp.int32)

    def exists(item):
        return jnp.where(item == 1, has_left, jnp.where(item == 3, jnp.logical_not(has_right), True))

    def has_far(item):
        return jnp.where(item == 1, has_left, has_right)

    def edge_copy(item, cut):
        flip = kind(item)
        j = slot_of(item, core)
        return pltpu.make_async_remote_copy(
            terms.at[item, cut], out.at[1 - flip, j], edge_ssem.at[item, cut], edge_rsem.at[1 - flip, j],
            device_id={"cuts": cut, "tile": jnp.where(flip == 1, left, right)},
        )

    def part_copy(item):
        return pltpu.make_async_remote_copy(
            terms.at[item, other], out.at[kind(item), slot_of(item, core)],
            part_ssem.at[item], part_rsem.at[item], device_id=partner,
        )

    def keep_copy(item):
        return pltpu.make_async_copy(
            terms.at[item, core], out.at[kind(item), slot_of(item, core)], keep_sem.at[item]
        )

    def work(item):
        flip = kind(item)
        j = slot_of(item, core)
        row = jnp.bitwise_and(index[flip, j], size - 1)
        column = index[flip, 8 + j]
        live = index[flip, 16 + j] > 0
        to_row = (rows == jnp.bitwise_and(lanes + row, size - 1)).astype(F32).astype(BF16)
        to_lane = (lanes == jnp.bitwise_and(rows + column, size - 1)).astype(F32).astype(BF16)

        def moved(value):
            moving = jnp.dot(value, to_lane, preferred_element_type=F32).astype(BF16)
            return jnp.dot(to_row, moving, preferred_element_type=F32)

        def shifted(value):
            high = value.astype(BF16)
            low = (value - high.astype(F32)).astype(BF16)
            return moved(high) + moved(low)

        for plane in (0, 1):
            psi0[plane] = shifted(probe[plane])
        own_copy(item).wait_recv()
        start = jnp.where(flip == 1, 0, column)
        stop = jnp.where(flip == 1, column, size)
        inside = (lanes >= start) & (lanes < stop)

        @pl.when(has_far(item))
        def _():
            for cut in (0, 1):
                pltpu.make_async_remote_copy(
                    send_left.at[0], far.at[item, cut], left_ssem.at[0], far_rsem.at[item, cut],
                    device_id={"cuts": cut, "tile": right},
                ).wait_recv()
                for plane in (0, 1):
                    window[cut, plane] = jnp.where(
                        inside, own[item, cut, plane].astype(F32), far[item, cut, plane].astype(F32)
                    )

        @pl.when(jnp.logical_not(has_far(item)))
        def _():
            for cut in (0, 1):
                for plane in (0, 1):
                    window[cut, plane] = jnp.where(inside, own[item, cut, plane].astype(F32), 0.0)

        @pl.when(flip == 1)
        def _():
            level_copy.wait_recv()
            measured[...] = level_far[...].astype(F32)

        @pl.when(flip == 0)
        def _():
            measured[...] = intensity[chosen[0, j]]

        real, imag = psi0[0], psi0[1]
        o_real, o_imag = window[0, 0], window[0, 1]
        real, imag = propagate(real * o_real - imag * o_imag, real * o_imag + imag * o_real, 0, 1.0)
        psi1[0] = real.astype(BF16)
        psi1[1] = imag.astype(BF16)
        real, imag = psi1[0].astype(F32), psi1[1].astype(F32)
        o_real, o_imag = window[1, 0], window[1, 1]
        real, imag = propagate(real * o_real - imag * o_imag, real * o_imag + imag * o_real, 1, 1.0)
        real, imag = real.astype(BF16).astype(F32), imag.astype(BF16).astype(F32)
        factor = 2.0 * (real * real + imag * imag - shifted(measured[...]))
        real = jnp.where(live, factor * real, 0.0)
        imag = jnp.where(live, factor * imag, 0.0)

        def emit(cut, wave, real, imag):
            w_real, w_imag = wave[0].astype(F32), wave[1].astype(F32)
            terms[item, cut, 0] = (w_real * real + w_imag * imag).astype(BF16)
            terms[item, cut, 1] = (w_real * imag - w_imag * real).astype(BF16)

            @pl.when(has_far(item))
            def _():
                edge_copy(item, cut).start()

        real, imag = propagate(real, imag, 1, -1.0)
        emit(1, psi1, real, imag)
        o_real, o_imag = window[1, 0], window[1, 1]
        real, imag = propagate(
            o_real * real + o_imag * imag, o_real * imag - o_imag * real, 0, -1.0
        )
        emit(0, psi0, real, imag)
        part_copy(item).start()
        keep_copy(item).start()

    @pl.loop(0, items)
    def _(item):
        @pl.when(exists(item))
        def _():
            work(item)

    phase_copy.wait_send()

    @pl.loop(0, items)
    def _(item):
        @pl.when(exists(item))
        def _():
            own_copy(item).wait_send()
            keep_copy(item).wait()
            part_copy(item).wait_send()
            part_copy(item).wait_recv()

            @pl.when(has_far(item))
            def _():
                edge_copy(item, 0).wait_send()
                edge_copy(item, 1).wait_send()

    def edge_arrives(kept, j):
        pltpu.make_async_remote_copy(
            terms.at[0, 0], out.at[kept, j], edge_ssem.at[0, 0], edge_rsem.at[kept, j],
            device_id={"cuts": core, "tile": right},
        ).wait_recv()

    @pl.when(has_right)
    def _():
        index_copy.wait_send()
        level_copy.wait_send()
        for half in (0, 1):
            right_copy(half).wait_send()
            edge_arrives(0, slots - 2 + half)

    @pl.when(has_left)
    def _():
        for j in range(slots - 2):
            left_copy(j).wait_send()
            edge_arrives(1, j)


def deposit_kernel(index, terms_ref, out_ref):
    block = pl.program_id(0)
    slots = terms_ref.shape[1]
    size = out_ref.shape[-1]
    rows = iota((size, size), 0)
    lanes = iota((size, size), 1)
    has_left = lax.axis_index("tile") > 0
    out_ref[...] = jnp.zeros_like(out_ref)

    for base in (0, 32):

        @pl.loop(0, slots)
        def _(j, base=base):
            row = index[base + j]
            column = index[base + 8 + j]
            first = lax.shift_right_logical(row, 8)
            start = jnp.bitwise_and(row, size - 1)
            live = index[base + 16 + j] > 0
            if base:
                live = live & has_left

            @pl.when(live & ((first == block) | (first + 1 == block)))
            def _():
                above = first == block
                low = jnp.where(above, start, 0)
                high = jnp.where(above, size, start)
                mask = (rows >= low) & (rows < high)
                mask = mask & ((lanes < column) if base else (lanes >= column))
                for plane in (0, 1):
                    out_ref[plane] += jnp.where(mask, terms_ref[base // 32, j, plane].astype(F32), 0.0)


def on_device(
    object_slices, probe_field, slice_phase, intensity, counts, chosen, row_offset, column_offset
):
    _, _, height, breadth = object_slices.shape
    size = probe_field.shape[-1]
    scan = row_offset.shape[1]
    slots = chosen.shape[1]
    items = 4
    forward, inverse = dft_tables(size)
    smem = pl.BlockSpec(memory_space=pltpu.SMEM)
    anywhere = pl.BlockSpec(memory_space=pl.ANY)
    stay = pl.BlockSpec(memory_space=pltpu.HBM)
    plane = (size, size)
    dma = pltpu.SemaphoreType.DMA
    operands = (
        chosen, row_offset, column_offset,
        object_slices.reshape(2, height // size, size, breadth), probe_field, slice_phase[0],
        intensity[0], jnp.asarray(forward), jnp.asarray(inverse),
    )
    index, terms = pl.pallas_call(
        slot_kernel,
        out_shape=(
            jax.ShapeDtypeStruct((64,), jnp.int32),
            jax.ShapeDtypeStruct((2, slots, 2) + plane, BF16),
        ),
        in_specs=[stay] * 10,
        out_specs=(smem, anywhere),
        scratch_shapes=[
            pltpu.VMEM((2, height // size) + plane, F32),
            pltpu.VMEM((2,) + plane, F32),
            pltpu.VMEM((2,) + plane, F32),
            pltpu.VMEM((2, 2) + plane, F32),
            pltpu.VMEM((scan,) + plane, F32),
            pltpu.VMEM((2 * size, 2 * size), BF16),
            pltpu.VMEM((2 * size, 2 * size), BF16),
            pltpu.VMEM((items, 2, 2) + plane, BF16),
            pltpu.VMEM((items, 2) + plane, BF16),
            pltpu.VMEM((items, 2, 2) + plane, BF16),
            pltpu.VMEM((slots - 2, 2) + plane, BF16),
            pltpu.VMEM((2, 2) + plane, BF16),
            pltpu.VMEM(plane, BF16),
            pltpu.VMEM(plane, BF16),
            pltpu.VMEM(plane, F32),
            pltpu.VMEM((items, 2, 2) + plane, BF16),
            pltpu.VMEM((2,) + plane, F32),
            pltpu.VMEM((2,) + plane, BF16),
            pltpu.VMEM((2, 2) + plane, F32),
            pltpu.VMEM((size, 2 * size), BF16),
            pltpu.VMEM((2 * size, size), BF16),
            pltpu.SMEM((2, 32), jnp.int32),
            pltpu.SMEM((1,), jnp.int32),
            pltpu.SMEM((1, slots), jnp.int32),
            pltpu.SMEM((1, scan), jnp.int32),
            pltpu.SMEM((1, scan), jnp.int32),
            dma((10,)),
            dma((2,)),
            dma((2,)),
            dma((2,)),
            dma((items,)),
            dma((items,)),
            dma((slots - 2,)),
            dma((2,)),
            dma((items, 2)),
            dma((items,)),
            dma((items,)),
            dma((items,)),
            dma((items, 2)),
            dma((2, slots)),
        ],
        compiler_params=pltpu.CompilerParams(
            collective_id=0, has_side_effects=True, vmem_limit_bytes=48 * 1024 * 1024
        ),
        name="slots",
    )(counts, *[pltpu.with_memory_space_constraint(operand, pltpu.HBM) for operand in operands])
    gradient = pl.pallas_call(
        deposit_kernel,
        grid_spec=pltpu.PrefetchScalarGridSpec(
            num_scalar_prefetch=1,
            grid=(height // size,),
            in_specs=[
                pl.BlockSpec(
                    (2, slots, 2) + plane,
                    lambda b, *_: (0, 0, 0, 0, 0),
                    pipeline_mode=pl.Buffered(1),
                )
            ],
            out_specs=pl.BlockSpec((2, size, breadth), lambda b, *_: (0, b, 0)),
        ),
        out_shape=jax.ShapeDtypeStruct((2, height, breadth), F32),
        compiler_params=pltpu.CompilerParams(vmem_limit_bytes=32 * 1024 * 1024),
        name="deposit",
    )(index, terms)
    return gradient[None]


def solution(mesh):
    return jax.shard_map(
        on_device,
        mesh=mesh,
        in_specs=(
            P("cuts", None, None, "tile"),
            P(),
            P("cuts", None, None),
            P("tile", None, None, None),
            P("tile"),
            P("tile", None),
            P("tile", None),
            P("tile", None),
        ),
        out_specs=P("cuts", None, None, "tile"),
        check_vma=False,
    )
```

```python
import jax
import jax.numpy as jnp
import numpy as np
from jax import lax
from jax.experimental import pallas as pl
from jax.experimental.pallas import tpu as pltpu
from jax.sharding import PartitionSpec as P

BF16 = jnp.bfloat16
F32 = jnp.float32


def dft_tables(length):
    index = np.arange(length, dtype=np.int32)
    product = index[:, None] * index[None, :] % length
    angle = product.astype(np.float32) * np.float32(2.0 * np.pi / length)
    scale = np.float32(length ** (-0.5))
    cosine = np.cos(angle) * scale
    sine = np.sin(angle) * scale
    forward = np.block([[cosine, -sine], [sine, cosine]])
    inverse = np.block([[cosine, sine], [-sine, cosine]])
    return forward.astype(BF16), inverse.astype(BF16)


def iota(shape, axis):
    return lax.broadcasted_iota(jnp.int32, shape, axis)


def slot_of(item, cut):
    return lax.rem(3 * cut + 4 * item, 6)


def slot_kernel(
    counts_hbm, chosen_hbm, row_hbm, column_hbm,
    obj_hbm, probe_hbm, phase_hbm, intensity_hbm, fwd_hbm, inv_hbm,
    index_out, out,
    obj, probe, phase, trig, intensity, fwd, inv,
    own, own_send, far, send_left, send_right, level_send, level_far, measured,
    terms, psi0, psi1, window, xbuf, ybuf,
    index, counts, chosen, row_offset, column_offset,
    in_sem, index_sem, phase_sem, level_ssem, level_rsem, own_ssem, own_rsem, left_ssem, right_ssem, far_rsem,
    keep_sem, part_ssem, part_rsem, edge_ssem, edge_rsem,
):
    slots = chosen.shape[1]
    kept = slots // 2
    size = probe.shape[-1]
    items = terms.shape[0]
    last_block = obj.shape[1] - 1
    core = lax.axis_index("cuts")
    tile = lax.axis_index("tile")
    tiles = lax.axis_size("tile")
    other = 1 - core
    right = lax.rem(tile + 1, tiles)
    left = lax.rem(tile + tiles - 1, tiles)
    has_left = tile > 0
    has_right = tile < tiles - 1
    partner = {"cuts": other, "tile": tile}

    def copy_in(source, target, number):
        return pltpu.make_async_copy(source, target, in_sem.at[number])

    scalars = [
        copy_in(counts_hbm, counts, 0),
        copy_in(chosen_hbm, chosen, 1),
        copy_in(row_hbm, row_offset, 2),
        copy_in(column_hbm, column_offset, 3),
    ]
    load_obj = copy_in(obj_hbm, obj, 4)
    load_phase = copy_in(phase_hbm, phase.at[core], 5)
    load_intensity = copy_in(intensity_hbm, intensity, 6)
    rest = [copy_in(probe_hbm, probe, 7), copy_in(fwd_hbm, fwd, 8), copy_in(inv_hbm, inv, 9)]
    for load in scalars + [load_obj, load_phase, load_intensity] + rest:
        load.start()

    for k in range(32):
        index[0, k] = 0

    @pl.when(tile == 0)
    def _():
        for k in range(32):
            index[1, k] = 0

    barrier = pltpu.get_barrier_semaphore()
    pl.semaphore_signal(barrier, inc=1, device_id=partner)
    for there, reached in ((left, has_left), (right, has_right)):

        @pl.when(reached)
        def _(there=there):
            for cut in (0, 1):
                pl.semaphore_signal(barrier, inc=1, device_id={"cuts": cut, "tile": there})

    for load in scalars:
        load.wait()
    for j in range(slots):
        q = chosen[0, j]
        index[0, j] = row_offset[0, q]
        index[0, 8 + j] = column_offset[0, q]
        index[0, 16 + j] = (j < counts[0]).astype(jnp.int32)

    rows = iota((size, size), 0)
    lanes = iota((size, size), 1)

    def fold(row, plane):
        block = lax.shift_right_logical(row, 8)
        after = jnp.minimum(block + 1, last_block)
        here = obj[plane, block]
        below = obj[plane, after]
        return jnp.where(rows >= jnp.bitwise_and(row, size - 1), here, below).astype(BF16)

    index_copy = pltpu.make_async_remote_copy(
        index.at[0], index.at[1], index_sem.at[0], index_sem.at[1],
        device_id={"cuts": core, "tile": right},
    )
    phase_copy = pltpu.make_async_remote_copy(
        phase.at[core], phase.at[core], phase_sem.at[0], phase_sem.at[1], device_id=partner
    )
    def level_copy(n):
        return pltpu.make_async_remote_copy(
            level_send.at[n], level_far.at[n], level_ssem.at[n], level_rsem.at[n],
            device_id={"cuts": core, "tile": right},
        )

    def right_copy(j):
        return pltpu.make_async_remote_copy(
            send_right.at[j - kept], far.at[j // 2, core],
            right_ssem.at[j - kept], far_rsem.at[j // 2, core],
            device_id={"cuts": j % 2, "tile": right},
        )

    def left_copy(j):
        return pltpu.make_async_remote_copy(
            send_left.at[j], far.at[j // 2, core], left_ssem.at[j], far_rsem.at[j // 2, core],
            device_id={"cuts": j % 2, "tile": left},
        )

    def own_copy(item):
        return pltpu.make_async_remote_copy(
            own_send.at[item], own.at[item, core], own_ssem.at[item], own_rsem.at[item],
            device_id=partner,
        )

    def kind(item, cut):
        return ((item < 3) & (slot_of(item, cut) >= kept)).astype(jnp.int32)

    def exists(item, cut):
        away = slot_of(item, cut) >= kept
        usual = (item < 3) & (jnp.logical_not(away) | has_left)
        return usual | ((item >= 3) & away & jnp.logical_not(has_right))

    def has_far(item, cut):
        return jnp.where(kind(item, cut) == 1, has_left, has_right)

    def near_windows(first, last, flip):
        @pl.loop(first, last)
        def _(item):
            @pl.when(exists(item, other) & (kind(item, other) == flip))
            def _():
                row = index[flip, slot_of(item, other)]
                for plane in (0, 1):
                    own_send[item, plane] = fold(row, plane)
                own_copy(item).start()

            @pl.when(exists(item, core) & (kind(item, core) == flip))
            def _():
                row = index[flip, slot_of(item, core)]
                for plane in (0, 1):
                    own[item, core, plane] = fold(row, plane)

    peers = 1 + 2 * has_left.astype(jnp.int32) + 2 * has_right.astype(jnp.int32)
    load_obj.wait()
    for plane in (0, 1):
        send_right[0, plane] = fold(index[0, kept], plane)
    load_intensity.wait()
    level_send[0] = intensity[chosen[0, 4 - core]].astype(BF16)
    level_send[1] = intensity[chosen[0, 5]].astype(BF16)
    pl.semaphore_wait(barrier, peers)

    @pl.when(has_right)
    def _():
        index_copy.start()

        @pl.when(core == 1)
        def _():
            level_copy(0).start()

        right_copy(kept).start()

        @pl.when(core == 0)
        def _():
            level_copy(0).start()

        for plane in (0, 1):
            send_right[1, plane] = fold(index[0, kept + 1], plane)
        right_copy(kept + 1).start()

        @pl.when(core == 1)
        def _():
            level_copy(1).start()

        for plane in (0, 1):
            send_right[2, plane] = fold(index[0, kept + 2], plane)
        right_copy(kept + 2).start()

    load_phase.wait()
    phase_copy.start()
    near_windows(0, 3, 0)

    @pl.when(has_left)
    def _():
        index_copy.wait_recv()
        for j in range(kept):
            for plane in (0, 1):
                send_left[j, plane] = fold(index[1, j], plane)
            left_copy(j).start()

    @pl.when(has_left)
    def _():
        near_windows(0, 3, 1)

    @pl.when(jnp.logical_not(has_right))
    def _():
        near_windows(3, items, 0)

    for k in range(32):
        index_out[k] = index[0, k]
        index_out[32 + k] = index[1, k]

    phase_copy.wait_recv()

    @pl.loop(0, 2 * size // 32)
    def _(k):
        cut = k // (size // 32)
        start = pl.multiple_of(lax.rem(k, size // 32) * 32, 32)
        angle = phase[cut, pl.ds(start, 32), :]
        trig[cut, 0, pl.ds(start, 32), :] = jnp.cos(angle)
        trig[cut, 1, pl.ds(start, 32), :] = jnp.sin(angle)

    for load in rest:
        load.wait()

    def stage(real, imag):
        xbuf[:, :size] = real.astype(BF16)
        xbuf[:, size:] = imag.astype(BF16)

    def transform(right_table, left_table):
        halfway = jnp.dot(xbuf[...], right_table[...], preferred_element_type=F32)
        ybuf[:size, :] = halfway[:, :size].astype(BF16)
        ybuf[size:, :] = halfway[:, size:].astype(BF16)
        field = jnp.dot(left_table[...], ybuf[...], preferred_element_type=F32)
        return field[:size], field[size:]

    def propagate(real, imag, cut, sign):
        stage(real, imag)
        real, imag = transform(fwd, inv)
        cosine = trig[cut, 0]
        sine = trig[cut, 1] * sign
        stage(real * cosine - imag * sine, real * sine + imag * cosine)
        return transform(inv, fwd)

    def edge_copy(item, cut):
        flip = kind(item, core)
        j = slot_of(item, core)
        return pltpu.make_async_remote_copy(
            terms.at[item, cut], out.at[1 - flip, j], edge_ssem.at[item, cut], edge_rsem.at[1 - flip, j],
            device_id={"cuts": cut, "tile": jnp.where(flip == 1, left, right)},
        )

    def part_copy(item):
        return pltpu.make_async_remote_copy(
            terms.at[item, other], out.at[kind(item, core), slot_of(item, core)],
            part_ssem.at[item], part_rsem.at[item], device_id=partner,
        )

    def keep_copy(item):
        return pltpu.make_async_copy(
            terms.at[item, core], out.at[kind(item, core), slot_of(item, core)], keep_sem.at[item]
        )

    def work(item):
        flip = kind(item, core)
        j = slot_of(item, core)
        row = jnp.bitwise_and(index[flip, j], size - 1)
        column = index[flip, 8 + j]
        live = index[flip, 16 + j] > 0
        to_row = (rows == jnp.bitwise_and(lanes + row, size - 1)).astype(F32).astype(BF16)
        to_lane = (lanes == jnp.bitwise_and(rows + column, size - 1)).astype(F32).astype(BF16)

        def moved(value):
            moving = jnp.dot(value, to_lane, preferred_element_type=F32).astype(BF16)
            return jnp.dot(to_row, moving, preferred_element_type=F32)

        def shifted(value):
            high = value.astype(BF16)
            low = (value - high.astype(F32)).astype(BF16)
            return moved(high) + moved(low)

        for plane in (0, 1):
            psi0[plane] = shifted(probe[plane])
        own_copy(item).wait_recv()
        start = jnp.where(flip == 1, 0, column)
        stop = jnp.where(flip == 1, column, size)
        inside = (lanes >= start) & (lanes < stop)

        @pl.when(has_far(item, core))
        def _():
            for cut in (0, 1):
                pltpu.make_async_remote_copy(
                    send_left.at[0], far.at[j // 2, cut], left_ssem.at[0], far_rsem.at[j // 2, cut],
                    device_id={"cuts": cut, "tile": right},
                ).wait_recv()
                for plane in (0, 1):
                    window[cut, plane] = jnp.where(
                        inside, own[item, cut, plane].astype(F32), far[j // 2, cut, plane].astype(F32)
                    )

        @pl.when(jnp.logical_not(has_far(item, core)))
        def _():
            for cut in (0, 1):
                for plane in (0, 1):
                    window[cut, plane] = jnp.where(inside, own[item, cut, plane].astype(F32), 0.0)

        @pl.when(flip == 1)
        def _():
            level_copy(j // 5).wait_recv()
            measured[...] = level_far[j // 5].astype(F32)

        @pl.when(flip == 0)
        def _():
            measured[...] = intensity[chosen[0, j]]

        real, imag = psi0[0], psi0[1]
        o_real, o_imag = window[0, 0], window[0, 1]
        real, imag = propagate(real * o_real - imag * o_imag, real * o_imag + imag * o_real, 0, 1.0)
        psi1[0] = real.astype(BF16)
        psi1[1] = imag.astype(BF16)
        real, imag = psi1[0].astype(F32), psi1[1].astype(F32)
        o_real, o_imag = window[1, 0], window[1, 1]
        real, imag = propagate(real * o_real - imag * o_imag, real * o_imag + imag * o_real, 1, 1.0)
        real, imag = real.astype(BF16).astype(F32), imag.astype(BF16).astype(F32)
        factor = 2.0 * (real * real + imag * imag - shifted(measured[...]))
        real = jnp.where(live, factor * real, 0.0)
        imag = jnp.where(live, factor * imag, 0.0)

        def emit(cut, wave, real, imag):
            w_real, w_imag = wave[0].astype(F32), wave[1].astype(F32)
            terms[item, cut, 0] = (w_real * real + w_imag * imag).astype(BF16)
            terms[item, cut, 1] = (w_real * imag - w_imag * real).astype(BF16)

            @pl.when(has_far(item, core))
            def _():
                edge_copy(item, cut).start()

        real, imag = propagate(real, imag, 1, -1.0)
        emit(1, psi1, real, imag)
        o_real, o_imag = window[1, 0], window[1, 1]
        real, imag = propagate(
            o_real * real + o_imag * imag, o_real * imag - o_imag * real, 0, -1.0
        )
        emit(0, psi0, real, imag)
        part_copy(item).start()
        keep_copy(item).start()

    @pl.loop(0, items)
    def _(turn):
        item = lax.rem(turn + 3, items)

        @pl.when(exists(item, core))
        def _():
            work(item)

    phase_copy.wait_send()

    @pl.loop(0, items)
    def _(item):
        @pl.when(exists(item, core))
        def _():
            keep_copy(item).wait()
            part_copy(item).wait_send()

            @pl.when(has_far(item, core))
            def _():
                edge_copy(item, 0).wait_send()
                edge_copy(item, 1).wait_send()

        @pl.when(exists(item, other))
        def _():
            own_copy(item).wait_send()
            part_copy(item).wait_recv()

    def edge_arrives(kept, j):
        pltpu.make_async_remote_copy(
            terms.at[0, 0], out.at[kept, j], edge_ssem.at[0, 0], edge_rsem.at[kept, j],
            device_id={"cuts": core, "tile": right},
        ).wait_recv()

    @pl.when(has_right)
    def _():
        index_copy.wait_send()
        level_copy(0).wait_send()

        @pl.when(core == 1)
        def _():
            level_copy(1).wait_send()

        for j in range(kept, slots):
            right_copy(j).wait_send()
            edge_arrives(0, j)

    @pl.when(has_left)
    def _():
        for j in range(kept):
            left_copy(j).wait_send()
            edge_arrives(1, j)


def deposit_kernel(index, terms, out_hbm, canvas, sem):
    slots = terms.shape[1]
    size = canvas.shape[-1]
    rows = iota((size, size), 0)
    lanes = iota((size, size), 1)
    has_left = lax.axis_index("tile") > 0

    def write(block):
        return pltpu.make_async_copy(canvas.at[block], out_hbm.at[:, block], sem.at[block])

    @pl.loop(0, canvas.shape[0])
    def _(block):
        canvas[block] = jnp.zeros(canvas.shape[1:], F32)
        for base in (0, 32):

            @pl.loop(0, slots)
            def _(j, base=base):
                row = index[base + j]
                column = index[base + 8 + j]
                first = lax.shift_right_logical(row, 8)
                begin = jnp.bitwise_and(row, size - 1)
                live = index[base + 16 + j] > 0
                if base:
                    live = live & has_left

                @pl.when(live & ((first == block) | (first + 1 == block)))
                def _():
                    above = first == block
                    low = jnp.where(above, begin, 0)
                    high = jnp.where(above, size, begin)
                    mask = (rows >= low) & (rows < high)
                    mask = mask & ((lanes < column) if base else (lanes >= column))
                    for plane in (0, 1):
                        added = jnp.where(mask, terms[base // 32, j, plane].astype(F32), 0.0)
                        canvas[block, plane] = canvas[block, plane] + added

        write(block).start()

    @pl.loop(0, canvas.shape[0])
    def _(block):
        write(block).wait()


def on_device(
    object_slices, probe_field, slice_phase, intensity, counts, chosen, row_offset, column_offset
):
    _, _, height, breadth = object_slices.shape
    size = probe_field.shape[-1]
    scan = row_offset.shape[1]
    slots = chosen.shape[1]
    items = slots
    forward, inverse = dft_tables(size)
    smem = pl.BlockSpec(memory_space=pltpu.SMEM)
    anywhere = pl.BlockSpec(memory_space=pl.ANY)
    stay = pl.BlockSpec(memory_space=pltpu.HBM)
    plane = (size, size)
    dma = pltpu.SemaphoreType.DMA
    operands = (
        chosen, row_offset, column_offset,
        object_slices.reshape(2, height // size, size, breadth), probe_field, slice_phase[0],
        intensity[0], jnp.asarray(forward), jnp.asarray(inverse),
    )
    index, terms = pl.pallas_call(
        slot_kernel,
        out_shape=(
            jax.ShapeDtypeStruct((64,), jnp.int32),
            jax.ShapeDtypeStruct((2, slots, 2) + plane, BF16),
        ),
        in_specs=[stay] * 10,
        out_specs=(smem, anywhere),
        scratch_shapes=[
            pltpu.VMEM((2, height // size) + plane, F32),
            pltpu.VMEM((2,) + plane, F32),
            pltpu.VMEM((2,) + plane, F32),
            pltpu.VMEM((2, 2) + plane, F32),
            pltpu.VMEM((scan,) + plane, F32),
            pltpu.VMEM((2 * size, 2 * size), BF16),
            pltpu.VMEM((2 * size, 2 * size), BF16),
            pltpu.VMEM((items, 2, 2) + plane, BF16),
            pltpu.VMEM((items, 2) + plane, BF16),
            pltpu.VMEM((3, 2, 2) + plane, BF16),
            pltpu.VMEM((slots // 2, 2) + plane, BF16),
            pltpu.VMEM((slots // 2, 2) + plane, BF16),
            pltpu.VMEM((2,) + plane, BF16),
            pltpu.VMEM((2,) + plane, BF16),
            pltpu.VMEM(plane, F32),
            pltpu.VMEM((items, 2, 2) + plane, BF16),
            pltpu.VMEM((2,) + plane, F32),
            pltpu.VMEM((2,) + plane, BF16),
            pltpu.VMEM((2, 2) + plane, F32),
            pltpu.VMEM((size, 2 * size), BF16),
            pltpu.VMEM((2 * size, size), BF16),
            pltpu.SMEM((2, 32), jnp.int32),
            pltpu.SMEM((1,), jnp.int32),
            pltpu.SMEM((1, slots), jnp.int32),
            pltpu.SMEM((1, scan), jnp.int32),
            pltpu.SMEM((1, scan), jnp.int32),
            dma((10,)),
            dma((2,)),
            dma((2,)),
            dma((2,)),
            dma((2,)),
            dma((items,)),
            dma((items,)),
            dma((slots // 2,)),
            dma((slots // 2,)),
            dma((3, 2)),
            dma((items,)),
            dma((items,)),
            dma((items,)),
            dma((items, 2)),
            dma((2, slots)),
        ],
        compiler_params=pltpu.CompilerParams(
            collective_id=0, has_side_effects=True, vmem_limit_bytes=48 * 1024 * 1024
        ),
        name="slots",
    )(counts, *[pltpu.with_memory_space_constraint(operand, pltpu.HBM) for operand in operands])
    gradient = pl.pallas_call(
        deposit_kernel,
        in_specs=[smem, pl.BlockSpec(memory_space=pltpu.VMEM)],
        out_specs=anywhere,
        out_shape=jax.ShapeDtypeStruct((2, height // size, size, breadth), F32),
        scratch_shapes=[
            pltpu.VMEM((height // size, 2) + plane, F32),
            dma((height // size,)),
        ],
        compiler_params=pltpu.CompilerParams(vmem_limit_bytes=32 * 1024 * 1024),
        name="deposit",
    )(index, terms)
    return gradient.reshape(1, 2, height, breadth)


def solution(mesh):
    return jax.shard_map(
        on_device,
        mesh=mesh,
        in_specs=(
            P("cuts", None, None, "tile"),
            P(),
            P("cuts", None, None),
            P("tile", None, None, None),
            P("tile"),
            P("tile", None),
            P("tile", None),
            P("tile", None),
        ),
        out_specs=P("cuts", None, None, "tile"),
        check_vma=False,
    )
```

```python
import jax
import jax.numpy as jnp
import numpy as np
from jax import lax
from jax.experimental import pallas as pl
from jax.experimental.pallas import tpu as pltpu
from jax.sharding import PartitionSpec as P

BF16 = jnp.bfloat16
F32 = jnp.float32


def dft_tables(length):
    index = np.arange(length, dtype=np.int32)
    product = index[:, None] * index[None, :] % length
    angle = product.astype(np.float32) * np.float32(2.0 * np.pi / length)
    scale = np.float32(length ** (-0.5))
    cosine = np.cos(angle) * scale
    sine = np.sin(angle) * scale
    forward = np.block([[cosine, -sine], [sine, cosine]])
    inverse = np.block([[cosine, sine], [-sine, cosine]])
    return forward.astype(BF16), inverse.astype(BF16)


def iota(shape, axis):
    return lax.broadcasted_iota(jnp.int32, shape, axis)


def slot_of(item, cut):
    return lax.rem(3 * cut + 4 * item, 6)


def slot_kernel(
    counts_hbm, chosen_hbm, row_hbm, column_hbm,
    obj_hbm, probe_hbm, phase_hbm, intensity_hbm, fwd_hbm, inv_hbm,
    index_out, out,
    obj, probe, phase, trig, intensity, fwd, inv,
    own, own_send, far, send_left, send_right, level_send, level_far, measured,
    terms, psi0, psi1, window, xbuf, ybuf,
    index, counts, chosen, row_offset, column_offset,
    in_sem, index_sem, phase_sem, level_ssem, level_rsem, own_ssem, own_rsem, left_ssem, right_ssem, far_rsem,
    keep_sem, part_ssem, part_rsem, edge_ssem, edge_rsem,
):
    slots = chosen.shape[1]
    kept = slots // 2
    size = probe.shape[-1]
    items = terms.shape[0]
    last_block = obj.shape[1] - 1
    core = lax.axis_index("cuts")
    tile = lax.axis_index("tile")
    tiles = lax.axis_size("tile")
    other = 1 - core
    right = lax.rem(tile + 1, tiles)
    left = lax.rem(tile + tiles - 1, tiles)
    has_left = tile > 0
    has_right = tile < tiles - 1
    partner = {"cuts": other, "tile": tile}

    def copy_in(source, target, number):
        return pltpu.make_async_copy(source, target, in_sem.at[number])

    scalars = [
        copy_in(counts_hbm, counts, 0),
        copy_in(chosen_hbm, chosen, 1),
        copy_in(row_hbm, row_offset, 2),
        copy_in(column_hbm, column_offset, 3),
    ]
    load_obj = copy_in(obj_hbm, obj, 4)
    load_phase = copy_in(phase_hbm, phase.at[core], 5)
    load_intensity = copy_in(intensity_hbm, intensity, 6)
    rest = [copy_in(probe_hbm, probe, 7), copy_in(fwd_hbm, fwd, 8), copy_in(inv_hbm, inv, 9)]
    @pl.when(tile == 0)
    def _():
        for k in range(32):
            index[1, k] = 0

    barrier = pltpu.get_barrier_semaphore()
    pl.semaphore_signal(barrier, inc=1, device_id=partner)
    for there, reached in ((left, has_left), (right, has_right)):

        @pl.when(reached)
        def _(there=there):
            for cut in (0, 1):
                pl.semaphore_signal(barrier, inc=1, device_id={"cuts": cut, "tile": there})

    for load in scalars + [load_obj, load_phase, load_intensity] + rest:
        load.start()

    for k in range(32):
        index[0, k] = 0
    for load in scalars:
        load.wait()
    for j in range(slots):
        q = chosen[0, j]
        index[0, j] = row_offset[0, q]
        index[0, 8 + j] = column_offset[0, q]
        index[0, 16 + j] = (j < counts[0]).astype(jnp.int32)

    rows = iota((size, size), 0)
    lanes = iota((size, size), 1)

    def fold(row, plane):
        block = lax.shift_right_logical(row, 8)
        after = jnp.minimum(block + 1, last_block)
        here = obj[plane, block]
        below = obj[plane, after]
        return jnp.where(rows >= jnp.bitwise_and(row, size - 1), here, below).astype(BF16)

    index_copy = pltpu.make_async_remote_copy(
        index.at[0], index.at[1], index_sem.at[0], index_sem.at[1],
        device_id={"cuts": core, "tile": right},
    )
    phase_copy = pltpu.make_async_remote_copy(
        phase.at[core], phase.at[core], phase_sem.at[0], phase_sem.at[1], device_id=partner
    )
    def level_copy(n):
        return pltpu.make_async_remote_copy(
            level_send.at[n], level_far.at[n], level_ssem.at[n], level_rsem.at[n],
            device_id={"cuts": core, "tile": right},
        )

    def right_copy(j):
        return pltpu.make_async_remote_copy(
            send_right.at[j - kept], far.at[j // 2, core],
            right_ssem.at[j - kept], far_rsem.at[j // 2, core],
            device_id={"cuts": j % 2, "tile": right},
        )

    def left_copy(j):
        return pltpu.make_async_remote_copy(
            send_left.at[j], far.at[j // 2, core], left_ssem.at[j], far_rsem.at[j // 2, core],
            device_id={"cuts": j % 2, "tile": left},
        )

    def own_copy(item):
        return pltpu.make_async_remote_copy(
            own_send.at[item], own.at[item, core], own_ssem.at[item], own_rsem.at[item],
            device_id=partner,
        )

    def kind(item, cut):
        return ((item < 3) & (slot_of(item, cut) >= kept)).astype(jnp.int32)

    def exists(item, cut):
        away = slot_of(item, cut) >= kept
        usual = (item < 3) & (jnp.logical_not(away) | has_left)
        return usual | ((item >= 3) & away & jnp.logical_not(has_right))

    def has_far(item, cut):
        return jnp.where(kind(item, cut) == 1, has_left, has_right)

    def near_windows(first, last, flip):
        @pl.loop(first, last)
        def _(item):
            @pl.when(exists(item, other) & (kind(item, other) == flip))
            def _():
                row = index[flip, slot_of(item, other)]
                for plane in (0, 1):
                    own_send[item, plane] = fold(row, plane)
                own_copy(item).start()

            @pl.when(exists(item, core) & (kind(item, core) == flip))
            def _():
                row = index[flip, slot_of(item, core)]
                for plane in (0, 1):
                    own[item, core, plane] = fold(row, plane)

    peers = 1 + 2 * has_left.astype(jnp.int32) + 2 * has_right.astype(jnp.int32)
    load_obj.wait()
    for plane in (0, 1):
        send_right[0, plane] = fold(index[0, kept], plane)
    load_intensity.wait()
    level_send[0] = intensity[chosen[0, 4 - core]].astype(BF16)
    level_send[1] = intensity[chosen[0, 5]].astype(BF16)
    pl.semaphore_wait(barrier, peers)

    @pl.when(has_right)
    def _():
        index_copy.start()

        @pl.when(core == 1)
        def _():
            level_copy(0).start()

        right_copy(kept).start()

        @pl.when(core == 0)
        def _():
            level_copy(0).start()

        for plane in (0, 1):
            send_right[1, plane] = fold(index[0, kept + 1], plane)
        right_copy(kept + 1).start()

        @pl.when(core == 1)
        def _():
            level_copy(1).start()

        for plane in (0, 1):
            send_right[2, plane] = fold(index[0, kept + 2], plane)
        right_copy(kept + 2).start()

    load_phase.wait()
    phase_copy.start()
    near_windows(0, 3, 0)

    @pl.when(has_left)
    def _():
        index_copy.wait_recv()
        for j in range(kept):
            for plane in (0, 1):
                send_left[j, plane] = fold(index[1, j], plane)
            left_copy(j).start()

    @pl.when(has_left)
    def _():
        near_windows(0, 3, 1)

    @pl.when(jnp.logical_not(has_right))
    def _():
        near_windows(3, items, 0)

    for base in (0, 1):
        for j in range(slots):
            row = index[base, j]
            live = index[base, 16 + j] > 0
            index_out[32 * base + j] = jnp.where(live, lax.shift_right_logical(row, 8), -9)
            index_out[32 * base + 8 + j] = jnp.bitwise_and(row, size - 1)
            index_out[32 * base + 16 + j] = index[base, 8 + j]
        for k in (6, 7, 14, 15, 22, 23, 24, 25, 26, 27, 28, 29, 30, 31):
            index_out[32 * base + k] = 0

    phase_copy.wait_recv()

    @pl.loop(0, 2 * size // 32)
    def _(k):
        cut = k // (size // 32)
        start = pl.multiple_of(lax.rem(k, size // 32) * 32, 32)
        angle = phase[cut, pl.ds(start, 32), :]
        trig[cut, 0, pl.ds(start, 32), :] = jnp.cos(angle)
        trig[cut, 1, pl.ds(start, 32), :] = jnp.sin(angle)

    for load in rest:
        load.wait()

    def stage(real, imag):
        xbuf[:, :size] = real.astype(BF16)
        xbuf[:, size:] = imag.astype(BF16)

    def transform(right_table, left_table):
        halfway = jnp.dot(xbuf[...], right_table[...], preferred_element_type=F32)
        ybuf[:size, :] = halfway[:, :size].astype(BF16)
        ybuf[size:, :] = halfway[:, size:].astype(BF16)
        field = jnp.dot(left_table[...], ybuf[...], preferred_element_type=F32)
        return field[:size], field[size:]

    def propagate(real, imag, cut, sign):
        stage(real, imag)
        real, imag = transform(fwd, inv)
        cosine = trig[cut, 0]
        sine = trig[cut, 1] * sign
        stage(real * cosine - imag * sine, real * sine + imag * cosine)
        return transform(inv, fwd)

    def edge_copy(item, cut):
        flip = kind(item, core)
        j = slot_of(item, core)
        return pltpu.make_async_remote_copy(
            terms.at[item, cut], out.at[1 - flip, j], edge_ssem.at[item, cut], edge_rsem.at[1 - flip, j],
            device_id={"cuts": cut, "tile": jnp.where(flip == 1, left, right)},
        )

    def part_copy(item):
        return pltpu.make_async_remote_copy(
            terms.at[item, other], out.at[kind(item, core), slot_of(item, core)],
            part_ssem.at[item], part_rsem.at[item], device_id=partner,
        )

    def keep_copy(item):
        return pltpu.make_async_copy(
            terms.at[item, core], out.at[kind(item, core), slot_of(item, core)], keep_sem.at[item]
        )

    def work(item):
        flip = kind(item, core)
        j = slot_of(item, core)
        row = jnp.bitwise_and(index[flip, j], size - 1)
        column = index[flip, 8 + j]
        live = index[flip, 16 + j] > 0
        to_row = (rows == jnp.bitwise_and(lanes + row, size - 1)).astype(F32).astype(BF16)
        to_lane = (lanes == jnp.bitwise_and(rows + column, size - 1)).astype(F32).astype(BF16)

        def moved(value):
            moving = jnp.dot(value, to_lane, preferred_element_type=F32).astype(BF16)
            return jnp.dot(to_row, moving, preferred_element_type=F32)

        def shifted(value):
            high = value.astype(BF16)
            low = (value - high.astype(F32)).astype(BF16)
            return moved(high) + moved(low)

        for plane in (0, 1):
            psi0[plane] = shifted(probe[plane])
        own_copy(item).wait_recv()
        start = jnp.where(flip == 1, 0, column)
        stop = jnp.where(flip == 1, column, size)
        inside = (lanes >= start) & (lanes < stop)

        @pl.when(has_far(item, core))
        def _():
            for cut in (0, 1):
                pltpu.make_async_remote_copy(
                    send_left.at[0], far.at[j // 2, cut], left_ssem.at[0], far_rsem.at[j // 2, cut],
                    device_id={"cuts": cut, "tile": right},
                ).wait_recv()
                for plane in (0, 1):
                    window[cut, plane] = jnp.where(
                        inside, own[item, cut, plane].astype(F32), far[j // 2, cut, plane].astype(F32)
                    )

        @pl.when(jnp.logical_not(has_far(item, core)))
        def _():
            for cut in (0, 1):
                for plane in (0, 1):
                    window[cut, plane] = jnp.where(inside, own[item, cut, plane].astype(F32), 0.0)

        @pl.when(flip == 1)
        def _():
            level_copy(j // 5).wait_recv()
            measured[...] = level_far[j // 5].astype(F32)

        @pl.when(flip == 0)
        def _():
            measured[...] = intensity[chosen[0, j]]

        real, imag = psi0[0], psi0[1]
        o_real, o_imag = window[0, 0], window[0, 1]
        real, imag = propagate(real * o_real - imag * o_imag, real * o_imag + imag * o_real, 0, 1.0)
        psi1[0] = real.astype(BF16)
        psi1[1] = imag.astype(BF16)
        real, imag = psi1[0].astype(F32), psi1[1].astype(F32)
        o_real, o_imag = window[1, 0], window[1, 1]
        real, imag = propagate(real * o_real - imag * o_imag, real * o_imag + imag * o_real, 1, 1.0)
        real, imag = real.astype(BF16).astype(F32), imag.astype(BF16).astype(F32)
        factor = 2.0 * (real * real + imag * imag - shifted(measured[...]))
        real = jnp.where(live, factor * real, 0.0)
        imag = jnp.where(live, factor * imag, 0.0)

        def emit(cut, wave, real, imag):
            w_real, w_imag = wave[0].astype(F32), wave[1].astype(F32)
            terms[item, cut, 0] = (w_real * real + w_imag * imag).astype(BF16)
            terms[item, cut, 1] = (w_real * imag - w_imag * real).astype(BF16)

            @pl.when(has_far(item, core))
            def _():
                edge_copy(item, cut).start()

        real, imag = propagate(real, imag, 1, -1.0)
        emit(1, psi1, real, imag)
        o_real, o_imag = window[1, 0], window[1, 1]
        real, imag = propagate(
            o_real * real + o_imag * imag, o_real * imag - o_imag * real, 0, -1.0
        )
        emit(0, psi0, real, imag)
        part_copy(item).start()
        keep_copy(item).start()

    @pl.loop(0, items)
    def _(turn):
        item = lax.rem(turn + 3, items)

        @pl.when(exists(item, core))
        def _():
            work(item)

    phase_copy.wait_send()

    @pl.loop(0, items)
    def _(item):
        @pl.when(exists(item, core))
        def _():
            keep_copy(item).wait()
            part_copy(item).wait_send()

            @pl.when(has_far(item, core))
            def _():
                edge_copy(item, 0).wait_send()
                edge_copy(item, 1).wait_send()

        @pl.when(exists(item, other))
        def _():
            own_copy(item).wait_send()
            part_copy(item).wait_recv()

    def edge_arrives(kept, j):
        pltpu.make_async_remote_copy(
            terms.at[0, 0], out.at[kept, j], edge_ssem.at[0, 0], edge_rsem.at[kept, j],
            device_id={"cuts": core, "tile": right},
        ).wait_recv()

    @pl.when(has_right)
    def _():
        index_copy.wait_send()
        level_copy(0).wait_send()

        @pl.when(core == 1)
        def _():
            level_copy(1).wait_send()

        for j in range(kept, slots):
            right_copy(j).wait_send()
            edge_arrives(0, j)

    @pl.when(has_left)
    def _():
        for j in range(kept):
            left_copy(j).wait_send()
            edge_arrives(1, j)


def deposit_kernel(index, terms, out_hbm, canvas, sem):
    slots = terms.shape[1]
    size = canvas.shape[-1]
    strip = 32
    rows = iota((strip, size), 0)
    lanes = iota((strip, size), 1)

    def write(block):
        return pltpu.make_async_copy(canvas.at[block], out_hbm.at[:, block], sem.at[block])

    @pl.loop(0, canvas.shape[0])
    def _(block):
        canvas[block] = jnp.zeros(canvas.shape[1:], F32)
        for base in (0, 1):
            for j in range(slots):
                below = block - index[32 * base + j]

                @pl.when((below == 0) | (below == 1))
                def _(base=base, j=j, below=below):
                    begin = index[32 * base + 8 + j]
                    column = index[32 * base + 16 + j]
                    low = jnp.where(below == 0, begin, 0)
                    high = jnp.where(below == 0, size, begin)
                    columns = (lanes < column) if base else (lanes >= column)

                    @pl.loop(lax.shift_right_logical(low, 5), lax.shift_right_logical(high + strip - 1, 5))
                    def _(k):
                        start = pl.multiple_of(k * strip, strip)
                        mask = columns & (rows >= low - start) & (rows < high - start)
                        here = pl.ds(start, strip)
                        for plane in (0, 1):
                            added = terms[base, j, plane, here, :].astype(F32)
                            canvas[block, plane, here, :] += jnp.where(mask, added, 0.0)

        write(block).start()

    @pl.loop(0, canvas.shape[0])
    def _(block):
        write(block).wait()


def on_device(
    object_slices, probe_field, slice_phase, intensity, counts, chosen, row_offset, column_offset
):
    _, _, height, breadth = object_slices.shape
    size = probe_field.shape[-1]
    scan = row_offset.shape[1]
    slots = chosen.shape[1]
    items = slots
    forward, inverse = dft_tables(size)
    smem = pl.BlockSpec(memory_space=pltpu.SMEM)
    anywhere = pl.BlockSpec(memory_space=pl.ANY)
    stay = pl.BlockSpec(memory_space=pltpu.HBM)
    plane = (size, size)
    dma = pltpu.SemaphoreType.DMA
    operands = (
        chosen, row_offset, column_offset,
        object_slices.reshape(2, height // size, size, breadth), probe_field, slice_phase[0],
        intensity[0], jnp.asarray(forward), jnp.asarray(inverse),
    )
    index, terms = pl.pallas_call(
        slot_kernel,
        out_shape=(
            jax.ShapeDtypeStruct((64,), jnp.int32),
            jax.ShapeDtypeStruct((2, slots, 2) + plane, BF16),
        ),
        in_specs=[stay] * 10,
        out_specs=(smem, anywhere),
        scratch_shapes=[
            pltpu.VMEM((2, height // size) + plane, F32),
            pltpu.VMEM((2,) + plane, F32),
            pltpu.VMEM((2,) + plane, F32),
            pltpu.VMEM((2, 2) + plane, F32),
            pltpu.VMEM((scan,) + plane, F32),
            pltpu.VMEM((2 * size, 2 * size), BF16),
            pltpu.VMEM((2 * size, 2 * size), BF16),
            pltpu.VMEM((items, 2, 2) + plane, BF16),
            pltpu.VMEM((items, 2) + plane, BF16),
            pltpu.VMEM((3, 2, 2) + plane, BF16),
            pltpu.VMEM((slots // 2, 2) + plane, BF16),
            pltpu.VMEM((slots // 2, 2) + plane, BF16),
            pltpu.VMEM((2,) + plane, BF16),
            pltpu.VMEM((2,) + plane, BF16),
            pltpu.VMEM(plane, F32),
            pltpu.VMEM((items, 2, 2) + plane, BF16),
            pltpu.VMEM((2,) + plane, F32),
            pltpu.VMEM((2,) + plane, BF16),
            pltpu.VMEM((2, 2) + plane, F32),
            pltpu.VMEM((size, 2 * size), BF16),
            pltpu.VMEM((2 * size, size), BF16),
            pltpu.SMEM((2, 32), jnp.int32),
            pltpu.SMEM((1,), jnp.int32),
            pltpu.SMEM((1, slots), jnp.int32),
            pltpu.SMEM((1, scan), jnp.int32),
            pltpu.SMEM((1, scan), jnp.int32),
            dma((10,)),
            dma((2,)),
            dma((2,)),
            dma((2,)),
            dma((2,)),
            dma((items,)),
            dma((items,)),
            dma((slots // 2,)),
            dma((slots // 2,)),
            dma((3, 2)),
            dma((items,)),
            dma((items,)),
            dma((items,)),
            dma((items, 2)),
            dma((2, slots)),
        ],
        compiler_params=pltpu.CompilerParams(
            collective_id=0, has_side_effects=True, vmem_limit_bytes=48 * 1024 * 1024
        ),
        name="slots",
    )(counts, *[pltpu.with_memory_space_constraint(operand, pltpu.HBM) for operand in operands])
    gradient = pl.pallas_call(
        deposit_kernel,
        in_specs=[smem, pl.BlockSpec(memory_space=pltpu.VMEM)],
        out_specs=anywhere,
        out_shape=jax.ShapeDtypeStruct((2, height // size, size, breadth), F32),
        scratch_shapes=[
            pltpu.VMEM((height // size, 2) + plane, F32),
            dma((height // size,)),
        ],
        compiler_params=pltpu.CompilerParams(vmem_limit_bytes=32 * 1024 * 1024),
        name="deposit",
    )(index, terms)
    return gradient.reshape(1, 2, height, breadth)


def solution(mesh):
    return jax.shard_map(
        on_device,
        mesh=mesh,
        in_specs=(
            P("cuts", None, None, "tile"),
            P(),
            P("cuts", None, None),
            P("tile", None, None, None),
            P("tile"),
            P("tile", None),
            P("tile", None),
            P("tile", None),
        ),
        out_specs=P("cuts", None, None, "tile"),
        check_vma=False,
    )
```

```python
import jax
import jax.numpy as jnp
import numpy as np
from jax import lax
from jax.experimental import pallas as pl
from jax.experimental.pallas import tpu as pltpu
from jax.sharding import PartitionSpec as P

BF16 = jnp.bfloat16
F32 = jnp.float32


def dft_tables(length):
    index = np.arange(length, dtype=np.int32)
    product = index[:, None] * index[None, :] % length
    angle = product.astype(np.float32) * np.float32(2.0 * np.pi / length)
    scale = np.float32(length ** (-0.5))
    cosine = np.cos(angle) * scale
    sine = np.sin(angle) * scale
    forward = np.block([[cosine, -sine], [sine, cosine]])
    inverse = np.block([[cosine, sine], [-sine, cosine]])
    return forward.astype(BF16), inverse.astype(BF16)


def iota(shape, axis):
    return lax.broadcasted_iota(jnp.int32, shape, axis)


def slot_of(item, cut):
    return lax.rem(3 * cut + 4 * item, 6)


def slot_kernel(
    counts_hbm, chosen_hbm, row_hbm, column_hbm,
    obj_hbm, probe_hbm, phase_hbm, intensity_hbm, fwd_hbm, inv_hbm,
    index_out, canvas, final,
    obj, probe, phase, trig, intensity, fwd, inv,
    own, own_send, far, send_left, send_right, level_send, level_far, measured,
    terms, pieces, psi0, psi1, field_, window, xbuf, ybuf,
    index, counts, chosen, row_offset, column_offset,
    in_sem, index_sem, phase_sem, level_ssem, level_rsem, own_ssem, own_rsem, left_ssem, right_ssem, far_rsem,
    keep_sem, part_ssem, part_rsem, edge_ssem, edge_rsem,
):
    slots = chosen.shape[1]
    kept = slots // 2
    size = probe.shape[-1]
    items = terms.shape[0]
    last_block = obj.shape[1] - 1
    core = lax.axis_index("cuts")
    tile = lax.axis_index("tile")
    tiles = lax.axis_size("tile")
    other = 1 - core
    right = lax.rem(tile + 1, tiles)
    left = lax.rem(tile + tiles - 1, tiles)
    has_left = tile > 0
    has_right = tile < tiles - 1
    partner = {"cuts": other, "tile": tile}

    def copy_in(source, target, number):
        return pltpu.make_async_copy(source, target, in_sem.at[number])

    scalars = [
        copy_in(counts_hbm, counts, 0),
        copy_in(chosen_hbm, chosen, 1),
        copy_in(row_hbm, row_offset, 2),
        copy_in(column_hbm, column_offset, 3),
    ]
    load_obj = copy_in(obj_hbm, obj, 4)
    load_phase = copy_in(phase_hbm, phase.at[core], 5)
    load_intensity = copy_in(intensity_hbm, intensity, 6)
    rest = [copy_in(probe_hbm, probe, 7), copy_in(fwd_hbm, fwd, 8), copy_in(inv_hbm, inv, 9)]
    @pl.when(tile == 0)
    def _():
        for k in range(32):
            index[1, k] = 0

    barrier = pltpu.get_barrier_semaphore()
    pl.semaphore_signal(barrier, inc=1, device_id=partner)
    for there, reached in ((left, has_left), (right, has_right)):

        @pl.when(reached)
        def _(there=there):
            for cut in (0, 1):
                pl.semaphore_signal(barrier, inc=1, device_id={"cuts": cut, "tile": there})

    for load in scalars + [load_obj, load_phase, load_intensity] + rest:
        load.start()

    for k in range(32):
        index[0, k] = 0
    for load in scalars:
        load.wait()
    for j in range(slots):
        q = chosen[0, j]
        index[0, j] = row_offset[0, q]
        index[0, 8 + j] = column_offset[0, q]
        index[0, 16 + j] = (j < counts[0]).astype(jnp.int32)

    rows = iota((size, size), 0)
    lanes = iota((size, size), 1)

    def fold(row, plane):
        block = lax.shift_right_logical(row, 8)
        after = jnp.minimum(block + 1, last_block)
        here = obj[plane, block]
        below = obj[plane, after]
        return jnp.where(rows >= jnp.bitwise_and(row, size - 1), here, below).astype(BF16)

    index_copy = pltpu.make_async_remote_copy(
        index.at[0], index.at[1], index_sem.at[0], index_sem.at[1],
        device_id={"cuts": core, "tile": right},
    )
    phase_copy = pltpu.make_async_remote_copy(
        phase.at[core], phase.at[core], phase_sem.at[0], phase_sem.at[1], device_id=partner
    )
    def level_copy(n):
        return pltpu.make_async_remote_copy(
            level_send.at[n], level_far.at[n], level_ssem.at[n], level_rsem.at[n],
            device_id={"cuts": core, "tile": right},
        )

    def right_copy(j):
        return pltpu.make_async_remote_copy(
            send_right.at[j - kept], far.at[j // 2, core],
            right_ssem.at[j - kept], far_rsem.at[j // 2, core],
            device_id={"cuts": j % 2, "tile": right},
        )

    def left_copy(j):
        return pltpu.make_async_remote_copy(
            send_left.at[j], far.at[j // 2, core], left_ssem.at[j], far_rsem.at[j // 2, core],
            device_id={"cuts": j % 2, "tile": left},
        )

    def own_copy(item):
        return pltpu.make_async_remote_copy(
            own_send.at[item], own.at[item, core], own_ssem.at[item], own_rsem.at[item],
            device_id=partner,
        )

    def kind(item, cut):
        return ((item < 3) & (slot_of(item, cut) >= kept)).astype(jnp.int32)

    def exists(item, cut):
        away = slot_of(item, cut) >= kept
        usual = (item < 3) & (jnp.logical_not(away) | has_left)
        return usual | ((item >= 3) & away & jnp.logical_not(has_right))

    def has_far(item, cut):
        return jnp.where(kind(item, cut) == 1, has_left, has_right)

    def near_windows(first, last, flip):
        @pl.loop(first, last)
        def _(item):
            @pl.when(exists(item, other) & (kind(item, other) == flip))
            def _():
                row = index[flip, slot_of(item, other)]
                for plane in (0, 1):
                    own_send[item, plane] = fold(row, plane)
                own_copy(item).start()

            @pl.when(exists(item, core) & (kind(item, core) == flip))
            def _():
                row = index[flip, slot_of(item, core)]
                for plane in (0, 1):
                    own[item, core, plane] = fold(row, plane)

    peers = 1 + 2 * has_left.astype(jnp.int32) + 2 * has_right.astype(jnp.int32)
    load_obj.wait()
    for plane in (0, 1):
        send_right[0, plane] = fold(index[0, kept], plane)
    load_intensity.wait()
    level_send[0] = intensity[chosen[0, 4 - core]].astype(BF16)
    level_send[1] = intensity[chosen[0, 5]].astype(BF16)
    pl.semaphore_wait(barrier, peers)

    @pl.when(has_right)
    def _():
        index_copy.start()

        @pl.when(core == 1)
        def _():
            level_copy(0).start()

        right_copy(kept).start()

        @pl.when(core == 0)
        def _():
            level_copy(0).start()

        for plane in (0, 1):
            send_right[1, plane] = fold(index[0, kept + 1], plane)
        right_copy(kept + 1).start()

        @pl.when(core == 1)
        def _():
            level_copy(1).start()

        for plane in (0, 1):
            send_right[2, plane] = fold(index[0, kept + 2], plane)
        right_copy(kept + 2).start()

    load_phase.wait()
    phase_copy.start()
    near_windows(0, 3, 0)

    @pl.when(has_left)
    def _():
        index_copy.wait_recv()
        for j in range(kept):
            for plane in (0, 1):
                send_left[j, plane] = fold(index[1, j], plane)
            left_copy(j).start()

    @pl.when(has_left)
    def _():
        near_windows(0, 3, 1)

    @pl.when(jnp.logical_not(has_right))
    def _():
        near_windows(3, items, 0)

    last_live = (index[1, 16 + kept - 1] > 0) & has_left
    index_out[0] = jnp.where(last_live, lax.shift_right_logical(index[1, kept - 1], 8), -9)
    index_out[1] = jnp.bitwise_and(index[1, kept - 1], size - 1)
    index_out[2] = index[1, 8 + kept - 1]
    for k in range(3, 8):
        index_out[k] = 0

    @pl.loop(0, canvas.shape[0])
    def _(block):
        canvas[block] = jnp.zeros(canvas.shape[1:], F32)

    phase_copy.wait_recv()

    @pl.loop(0, 2 * size // 32)
    def _(k):
        cut = k // (size // 32)
        start = pl.multiple_of(lax.rem(k, size // 32) * 32, 32)
        angle = phase[cut, pl.ds(start, 32), :]
        trig[cut, 0, pl.ds(start, 32), :] = jnp.cos(angle)
        trig[cut, 1, pl.ds(start, 32), :] = jnp.sin(angle)

    for load in rest:
        load.wait()

    strip = 256

    def transform(right_table, left_table, finish):
        for start in range(0, size, strip):
            halfway = jnp.dot(
                xbuf[start:start + strip, :], right_table[...], preferred_element_type=F32
            ).astype(BF16)
            ybuf[start:start + strip, :] = halfway[:, :size]
            ybuf[size + start:size + start + strip, :] = halfway[:, size:]
        for start in range(0, size, strip):
            real = jnp.dot(
                left_table[start:start + strip, :], ybuf[...], preferred_element_type=F32
            )
            imag = jnp.dot(
                left_table[size + start:size + start + strip, :], ybuf[...], preferred_element_type=F32
            )
            finish(slice(start, start + strip), real, imag)

    def put(here, real, imag):
        xbuf[here, :size] = real.astype(BF16)
        xbuf[here, size:] = imag.astype(BF16)

    def propagate(field, cut, sign, finish):
        for start in range(0, size, strip):
            here = slice(start, start + strip)
            put(here, *field(here))

        def turn(here, real, imag):
            cosine = trig[cut, 0, here, :]
            sine = trig[cut, 1, here, :] * sign
            put(here, real * cosine - imag * sine, real * sine + imag * cosine)

        transform(fwd, inv, turn)
        transform(inv, fwd, finish)

    def edge_copy(item, cut):
        flip = kind(item, core)
        j = slot_of(item, core)
        return pltpu.make_async_remote_copy(
            terms.at[item, cut], pieces.at[1 - flip, j], edge_ssem.at[item, cut], edge_rsem.at[1 - flip, j],
            device_id={"cuts": cut, "tile": jnp.where(flip == 1, left, right)},
        )

    def final_copy(item, cut):
        return pltpu.make_async_remote_copy(
            terms.at[item, cut], final, edge_ssem.at[item, cut], edge_rsem.at[1, kept - 1],
            device_id={"cuts": cut, "tile": right},
        )

    def is_final(item):
        return (item < 3) & (slot_of(item, core) == kept - 1)

    def send_edge(item, cut):
        @pl.when(has_far(item, core) & is_final(item))
        def _():
            final_copy(item, cut).start()

        @pl.when(has_far(item, core) & jnp.logical_not(is_final(item)))
        def _():
            edge_copy(item, cut).start()

    def part_copy(item):
        return pltpu.make_async_remote_copy(
            terms.at[item, other], pieces.at[kind(item, core), slot_of(item, core)],
            part_ssem.at[item], part_rsem.at[item], device_id=partner,
        )

    def keep_copy(item):
        return pltpu.make_async_copy(
            terms.at[item, core], pieces.at[kind(item, core), slot_of(item, core)], keep_sem.at[item]
        )

    def work(item):
        flip = kind(item, core)
        j = slot_of(item, core)
        row = jnp.bitwise_and(index[flip, j], size - 1)
        column = index[flip, 8 + j]
        live = index[flip, 16 + j] > 0
        to_row = (rows == jnp.bitwise_and(lanes + row, size - 1)).astype(F32).astype(BF16)
        to_lane = (lanes == jnp.bitwise_and(rows + column, size - 1)).astype(F32).astype(BF16)

        def moved(value):
            moving = jnp.dot(value, to_lane, preferred_element_type=F32).astype(BF16)
            return jnp.dot(to_row, moving, preferred_element_type=F32)

        def shifted(value):
            high = value.astype(BF16)
            low = (value - high.astype(F32)).astype(BF16)
            return moved(high) + moved(low)

        for plane in (0, 1):
            psi0[plane] = shifted(probe[plane])
        own_copy(item).wait_recv()
        start = jnp.where(flip == 1, 0, column)
        stop = jnp.where(flip == 1, column, size)
        inside = (lanes >= start) & (lanes < stop)

        @pl.when(has_far(item, core))
        def _():
            for cut in (0, 1):
                pltpu.make_async_remote_copy(
                    send_left.at[0], far.at[j // 2, cut], left_ssem.at[0], far_rsem.at[j // 2, cut],
                    device_id={"cuts": cut, "tile": right},
                ).wait_recv()
                for plane in (0, 1):
                    window[cut, plane] = jnp.where(
                        inside, own[item, cut, plane].astype(F32), far[j // 2, cut, plane].astype(F32)
                    )

        @pl.when(jnp.logical_not(has_far(item, core)))
        def _():
            for cut in (0, 1):
                for plane in (0, 1):
                    window[cut, plane] = jnp.where(inside, own[item, cut, plane].astype(F32), 0.0)

        @pl.when(flip == 1)
        def _():
            level_copy(j // 5).wait_recv()
            measured[...] = level_far[j // 5].astype(F32)

        @pl.when(flip == 0)
        def _():
            measured[...] = intensity[chosen[0, j]]

        measured[...] = shifted(measured[...])

        def enter(wave, cut):
            def field(here):
                real, imag = wave[0, here, :].astype(F32), wave[1, here, :].astype(F32)
                o_real, o_imag = window[cut, 0, here, :], window[cut, 1, here, :]
                return real * o_real - imag * o_imag, real * o_imag + imag * o_real
            return field

        def keep(here, real, imag):
            psi1[0, here, :] = real.astype(BF16)
            psi1[1, here, :] = imag.astype(BF16)

        propagate(enter(psi0, 0), 0, 1.0, keep)

        def residual(here, real, imag):
            real, imag = real.astype(BF16).astype(F32), imag.astype(BF16).astype(F32)
            factor = 2.0 * (real * real + imag * imag - measured[here, :])
            field_[0, here, :] = jnp.where(live, factor * real, 0.0)
            field_[1, here, :] = jnp.where(live, factor * imag, 0.0)

        propagate(enter(psi1, 1), 1, 1.0, residual)

        def stored(here):
            return field_[0, here, :], field_[1, here, :]

        def emit(cut, wave, onward):
            def finish(here, real, imag):
                w_real, w_imag = wave[0, here, :].astype(F32), wave[1, here, :].astype(F32)
                terms[item, cut, 0, here, :] = (w_real * real + w_imag * imag).astype(BF16)
                terms[item, cut, 1, here, :] = (w_real * imag - w_imag * real).astype(BF16)
                if onward:
                    o_real, o_imag = window[cut, 0, here, :], window[cut, 1, here, :]
                    field_[0, here, :] = o_real * real + o_imag * imag
                    field_[1, here, :] = o_real * imag - o_imag * real
            return finish

        propagate(stored, 1, -1.0, emit(1, psi1, True))

        send_edge(item, 1)

        propagate(stored, 0, -1.0, emit(0, psi0, False))

        send_edge(item, 0)

        part_copy(item).start()
        keep_copy(item).start()

    @pl.loop(0, items)
    def _(turn):
        item = lax.rem(turn + 3, items)

        @pl.when(exists(item, core))
        def _():
            work(item)

    phase_copy.wait_send()

    @pl.loop(0, items)
    def _(item):
        @pl.when(exists(item, core))
        def _():
            keep_copy(item).wait()
            part_copy(item).wait_send()

        @pl.when(exists(item, other))
        def _():
            own_copy(item).wait_send()
            part_copy(item).wait_recv()

    strip = 64
    strip_rows = iota((strip, size), 0)
    strip_lanes = iota((strip, size), 1)

    def add_in(base, j):
        row = index[base, j]
        first = lax.shift_right_logical(row, 8)
        begin = jnp.bitwise_and(row, size - 1)
        column = index[base, 8 + j]
        columns = (strip_lanes < column) if base else (strip_lanes >= column)

        @pl.loop(0, canvas.shape[0])
        def _(block):
            below = block - first
            low = jnp.where(below == 0, begin, jnp.where(below == 1, 0, size))
            high = jnp.where(below == 0, size, begin)
            for start in range(0, size, strip):
                mask = columns & (strip_rows >= low - start) & (strip_rows < high - start)
                here = slice(start, start + strip)
                for plane in (0, 1):
                    added = pieces[base, j, plane, here, :].astype(F32)
                    canvas[block, plane, here, :] += jnp.where(mask, added, 0.0)

    def edge_arrives(base, j):
        pltpu.make_async_remote_copy(
            terms.at[0, 0], pieces.at[base, j], edge_ssem.at[0, 0], edge_rsem.at[base, j],
            device_id={"cuts": core, "tile": right},
        ).wait_recv()

    for j in range(kept):
        add_in(0, j)

    @pl.when(has_left)
    def _():
        for j in range(kept, slots):
            add_in(1, j)

    for j in range(kept):

        @pl.when(has_right)
        def _(j=j):
            edge_arrives(0, kept + j)

        add_in(0, kept + j)
        if j < kept - 1:

            @pl.when(has_left)
            def _(j=j):
                edge_arrives(1, j)
                add_in(1, j)

    @pl.loop(0, 3)
    def _(item):
        @pl.when(exists(item, core) & has_far(item, core))
        def _():
            for cut in (0, 1):
                edge_copy(item, cut).wait_send()

    @pl.when(has_right)
    def _():
        index_copy.wait_send()
        level_copy(0).wait_send()

        @pl.when(core == 1)
        def _():
            level_copy(1).wait_send()

        for j in range(kept, slots):
            right_copy(j).wait_send()

    @pl.when(has_left)
    def _():
        for j in range(kept):
            left_copy(j).wait_send()
        final_copy(0, 0).wait_recv()


def deposit_kernel(index_in, canvas, final, out_hbm, summed, index, index_sem, sem):
    size = final.shape[-1]
    rows = iota((size, size), 0)
    lanes = iota((size, size), 1)
    fetch = pltpu.make_async_copy(index_in, index, index_sem)
    fetch.start()
    fetch.wait()
    first, begin, column = index[0], index[1], index[2]

    @pl.loop(0, canvas.shape[0])
    def _(block):
        below = block - first
        touched = (below == 0) | (below == 1)

        @pl.when(jnp.logical_not(touched))
        def _():
            pltpu.make_async_copy(canvas.at[block], out_hbm.at[:, block], sem.at[block]).start()

        @pl.when(touched)
        def _():
            mask = (rows >= jnp.where(below == 0, begin, 0)) & (lanes < column)
            mask = mask & (rows < jnp.where(below == 0, size, begin))
            for plane in (0, 1):
                added = jnp.where(mask, final[plane].astype(F32), 0.0)
                summed[below, plane] = canvas[block, plane] + added
            pltpu.make_async_copy(summed.at[below], out_hbm.at[:, block], sem.at[block]).start()

    @pl.loop(0, canvas.shape[0])
    def _(block):
        pltpu.make_async_copy(canvas.at[block], out_hbm.at[:, block], sem.at[block]).wait()


def on_device(
    object_slices, probe_field, slice_phase, intensity, counts, chosen, row_offset, column_offset
):
    _, _, height, breadth = object_slices.shape
    size = probe_field.shape[-1]
    scan = row_offset.shape[1]
    slots = chosen.shape[1]
    items = slots
    forward, inverse = dft_tables(size)
    smem = pl.BlockSpec(memory_space=pltpu.SMEM)
    anywhere = pl.BlockSpec(memory_space=pl.ANY)
    stay = pl.BlockSpec(memory_space=pltpu.HBM)
    plane = (size, size)
    dma = pltpu.SemaphoreType.DMA
    operands = (
        chosen, row_offset, column_offset,
        object_slices.reshape(2, height // size, size, breadth), probe_field, slice_phase[0],
        intensity[0], jnp.asarray(forward), jnp.asarray(inverse),
    )
    index, canvas, final = pl.pallas_call(
        slot_kernel,
        out_shape=(
            jax.ShapeDtypeStruct((8,), jnp.int32),
            jax.ShapeDtypeStruct((height // size, 2) + plane, F32),
            jax.ShapeDtypeStruct((2,) + plane, BF16),
        ),
        in_specs=[stay] * 10,
        out_specs=(smem, pl.BlockSpec(memory_space=pltpu.VMEM), anywhere),
        scratch_shapes=[
            pltpu.VMEM((2, height // size) + plane, F32),
            pltpu.VMEM((2,) + plane, F32),
            pltpu.VMEM((2,) + plane, F32),
            pltpu.VMEM((2, 2) + plane, F32),
            pltpu.VMEM((scan,) + plane, F32),
            pltpu.VMEM((2 * size, 2 * size), BF16),
            pltpu.VMEM((2 * size, 2 * size), BF16),
            pltpu.VMEM((items, 2, 2) + plane, BF16),
            pltpu.VMEM((items, 2) + plane, BF16),
            pltpu.VMEM((3, 2, 2) + plane, BF16),
            pltpu.VMEM((slots // 2, 2) + plane, BF16),
            pltpu.VMEM((slots // 2, 2) + plane, BF16),
            pltpu.VMEM((2,) + plane, BF16),
            pltpu.VMEM((2,) + plane, BF16),
            pltpu.VMEM(plane, F32),
            pltpu.VMEM((items, 2, 2) + plane, BF16),
            pltpu.VMEM((2, slots, 2) + plane, BF16),
            pltpu.VMEM((2,) + plane, F32),
            pltpu.VMEM((2,) + plane, BF16),
            pltpu.VMEM((2,) + plane, F32),
            pltpu.VMEM((2, 2) + plane, F32),
            pltpu.VMEM((size, 2 * size), BF16),
            pltpu.VMEM((2 * size, size), BF16),
            pltpu.SMEM((2, 32), jnp.int32),
            pltpu.SMEM((1,), jnp.int32),
            pltpu.SMEM((1, slots), jnp.int32),
            pltpu.SMEM((1, scan), jnp.int32),
            pltpu.SMEM((1, scan), jnp.int32),
            dma((10,)),
            dma((2,)),
            dma((2,)),
            dma((2,)),
            dma((2,)),
            dma((items,)),
            dma((items,)),
            dma((slots // 2,)),
            dma((slots // 2,)),
            dma((3, 2)),
            dma((items,)),
            dma((items,)),
            dma((items,)),
            dma((items, 2)),
            dma((2, slots)),
        ],
        compiler_params=pltpu.CompilerParams(
            collective_id=0, has_side_effects=True, vmem_limit_bytes=48 * 1024 * 1024
        ),
        name="slots",
    )(counts, *[pltpu.with_memory_space_constraint(operand, pltpu.HBM) for operand in operands])
    gradient = pl.pallas_call(
        deposit_kernel,
        in_specs=[anywhere] + [pl.BlockSpec(memory_space=pltpu.VMEM)] * 2,
        out_specs=anywhere,
        out_shape=jax.ShapeDtypeStruct((2, height // size, size, breadth), F32),
        scratch_shapes=[
            pltpu.VMEM((2, 2) + plane, F32),
            pltpu.SMEM((8,), jnp.int32),
            pltpu.SemaphoreType.DMA,
            dma((height // size,)),
        ],
        compiler_params=pltpu.CompilerParams(vmem_limit_bytes=16 * 1024 * 1024),
        name="deposit",
    )(index, canvas, final)
    return gradient.reshape(1, 2, height, breadth)


def solution(mesh):
    return jax.shard_map(
        on_device,
        mesh=mesh,
        in_specs=(
            P("cuts", None, None, "tile"),
            P(),
            P("cuts", None, None),
            P("tile", None, None, None),
            P("tile"),
            P("tile", None),
            P("tile", None),
            P("tile", None),
        ),
        out_specs=P("cuts", None, None, "tile"),
        check_vma=False,
    )
```

```python
import jax
import jax.numpy as jnp
import numpy as np
from jax import lax
from jax.experimental import pallas as pl
from jax.experimental.pallas import tpu as pltpu
from jax.sharding import PartitionSpec as P

BF16 = jnp.bfloat16
F32 = jnp.float32


def dft_tables(length):
    index = np.arange(length, dtype=np.int32)
    product = index[:, None] * index[None, :] % length
    angle = product.astype(np.float32) * np.float32(2.0 * np.pi / length)
    scale = np.float32(length ** (-0.5))
    cosine = np.cos(angle) * scale
    sine = np.sin(angle) * scale
    forward = np.block([[cosine, -sine], [sine, cosine]])
    inverse = np.block([[cosine, sine], [-sine, cosine]])
    return forward.astype(BF16), inverse.astype(BF16)


def iota(shape, axis):
    return lax.broadcasted_iota(jnp.int32, shape, axis)


def slot_of(item, cut):
    return lax.rem(3 * cut + 4 * item, 6)


def slot_kernel(
    counts_hbm, chosen_hbm, row_hbm, column_hbm,
    obj_hbm, probe_hbm, phase_hbm, intensity_hbm, fwd_hbm, inv_hbm,
    index_out, canvas, final,
    obj, probe, phase, trig, intensity, fwd, inv,
    own, own_send, far, send_left, send_right, level_send, level_far, measured,
    terms, pieces, psi0, psi1, field_, window, xbuf, ybuf,
    index, counts, chosen, row_offset, column_offset,
    in_sem, index_sem, phase_sem, level_ssem, level_rsem, own_ssem, own_rsem, left_ssem, right_ssem, far_rsem,
    keep_sem, part_ssem, part_rsem, edge_ssem, edge_rsem,
):
    slots = chosen.shape[1]
    kept = slots // 2
    size = probe.shape[-1]
    items = terms.shape[0]
    last_block = obj.shape[1] - 1
    core = lax.axis_index("cuts")
    tile = lax.axis_index("tile")
    tiles = lax.axis_size("tile")
    other = 1 - core
    right = lax.rem(tile + 1, tiles)
    left = lax.rem(tile + tiles - 1, tiles)
    has_left = tile > 0
    has_right = tile < tiles - 1
    partner = {"cuts": other, "tile": tile}

    def copy_in(source, target, number):
        return pltpu.make_async_copy(source, target, in_sem.at[number])

    scalars = [
        copy_in(counts_hbm, counts, 0),
        copy_in(chosen_hbm, chosen, 1),
        copy_in(row_hbm, row_offset, 2),
        copy_in(column_hbm, column_offset, 3),
    ]
    load_obj = copy_in(obj_hbm, obj, 4)
    load_phase = copy_in(phase_hbm, phase.at[core], 5)
    load_intensity = copy_in(intensity_hbm, intensity, 6)
    rest = [copy_in(probe_hbm, probe, 7), copy_in(fwd_hbm, fwd, 8), copy_in(inv_hbm, inv, 9)]
    @pl.when(tile == 0)
    def _():
        for k in range(32):
            index[1, k] = 0

    barrier = pltpu.get_barrier_semaphore()
    pl.semaphore_signal(barrier, inc=1, device_id=partner)
    for there, reached in ((left, has_left), (right, has_right)):

        @pl.when(reached)
        def _(there=there):
            for cut in (0, 1):
                pl.semaphore_signal(barrier, inc=1, device_id={"cuts": cut, "tile": there})

    for load in scalars + [load_obj, load_phase, load_intensity] + rest:
        load.start()

    for k in range(32):
        index[0, k] = 0
    for load in scalars:
        load.wait()
    for j in range(slots):
        q = chosen[0, j]
        index[0, j] = row_offset[0, q]
        index[0, 8 + j] = column_offset[0, q]
        index[0, 16 + j] = (j < counts[0]).astype(jnp.int32)

    rows = iota((size, size), 0)
    lanes = iota((size, size), 1)

    def fold(row, plane):
        block = lax.shift_right_logical(row, 8)
        after = jnp.minimum(block + 1, last_block)
        here = obj[plane, block]
        below = obj[plane, after]
        return jnp.where(rows >= jnp.bitwise_and(row, size - 1), here, below).astype(BF16)

    index_copy = pltpu.make_async_remote_copy(
        index.at[0], index.at[1], index_sem.at[0], index_sem.at[1],
        device_id={"cuts": core, "tile": right},
    )
    phase_copy = pltpu.make_async_remote_copy(
        phase.at[core], phase.at[core], phase_sem.at[0], phase_sem.at[1], device_id=partner
    )
    def level_copy(n):
        return pltpu.make_async_remote_copy(
            level_send.at[n], level_far.at[n], level_ssem.at[n], level_rsem.at[n],
            device_id={"cuts": core, "tile": right},
        )

    def right_copy(j):
        return pltpu.make_async_remote_copy(
            send_right.at[j - kept], far.at[j // 2, core],
            right_ssem.at[j - kept], far_rsem.at[j // 2, core],
            device_id={"cuts": j % 2, "tile": right},
        )

    def left_copy(j):
        return pltpu.make_async_remote_copy(
            send_left.at[j], far.at[j // 2, core], left_ssem.at[j], far_rsem.at[j // 2, core],
            device_id={"cuts": j % 2, "tile": left},
        )

    def own_copy(item):
        return pltpu.make_async_remote_copy(
            own_send.at[item], own.at[item, core], own_ssem.at[item], own_rsem.at[item],
            device_id=partner,
        )

    def kind(item, cut):
        return ((item < 3) & (slot_of(item, cut) >= kept)).astype(jnp.int32)

    def exists(item, cut):
        away = slot_of(item, cut) >= kept
        usual = (item < 3) & (jnp.logical_not(away) | has_left)
        return usual | ((item >= 3) & away & jnp.logical_not(has_right))

    def has_far(item, cut):
        return jnp.where(kind(item, cut) == 1, has_left, has_right)

    def near_windows(first, last, flip):
        @pl.loop(first, last)
        def _(item):
            @pl.when(exists(item, other) & (kind(item, other) == flip))
            def _():
                row = index[flip, slot_of(item, other)]
                for plane in (0, 1):
                    own_send[item, plane] = fold(row, plane)
                own_copy(item).start()

            @pl.when(exists(item, core) & (kind(item, core) == flip))
            def _():
                row = index[flip, slot_of(item, core)]
                for plane in (0, 1):
                    own[item, core, plane] = fold(row, plane)

    peers = 1 + 2 * has_left.astype(jnp.int32) + 2 * has_right.astype(jnp.int32)
    load_obj.wait()
    for plane in (0, 1):
        send_right[0, plane] = fold(index[0, kept], plane)
    load_intensity.wait()
    level_send[0] = intensity[chosen[0, 4 - core]].astype(BF16)
    level_send[1] = intensity[chosen[0, 5]].astype(BF16)
    pl.semaphore_wait(barrier, peers)

    @pl.when(has_right)
    def _():
        index_copy.start()

        @pl.when(core == 1)
        def _():
            level_copy(0).start()

        right_copy(kept).start()

        @pl.when(core == 0)
        def _():
            level_copy(0).start()

        for plane in (0, 1):
            send_right[1, plane] = fold(index[0, kept + 1], plane)
        right_copy(kept + 1).start()

        @pl.when(core == 1)
        def _():
            level_copy(1).start()

        for plane in (0, 1):
            send_right[2, plane] = fold(index[0, kept + 2], plane)
        right_copy(kept + 2).start()

    load_phase.wait()
    phase_copy.start()
    near_windows(0, 3, 0)

    @pl.when(has_left)
    def _():
        index_copy.wait_recv()
        for j in range(kept):
            for plane in (0, 1):
                send_left[j, plane] = fold(index[1, j], plane)
            left_copy(j).start()

    @pl.when(has_left)
    def _():
        near_windows(0, 3, 1)

    @pl.when(jnp.logical_not(has_right))
    def _():
        near_windows(3, items, 0)

    last_live = (index[1, 16 + kept - 1] > 0) & has_left
    placed = (
        jnp.where(last_live, lax.shift_right_logical(index[1, kept - 1], 8), -9),
        jnp.bitwise_and(index[1, kept - 1], size - 1),
        index[1, 8 + kept - 1],
    )
    for k in range(3):
        index_out[k] = jnp.full(index_out.shape[1:], placed[k], jnp.int32).astype(F32)

    @pl.loop(0, canvas.shape[0])
    def _(block):
        canvas[block] = jnp.zeros(canvas.shape[1:], F32)

    phase_copy.wait_recv()

    @pl.loop(0, 2 * size // 32)
    def _(k):
        cut = k // (size // 32)
        start = pl.multiple_of(lax.rem(k, size // 32) * 32, 32)
        angle = phase[cut, pl.ds(start, 32), :]
        trig[cut, 0, pl.ds(start, 32), :] = jnp.cos(angle)
        trig[cut, 1, pl.ds(start, 32), :] = jnp.sin(angle)

    for load in rest:
        load.wait()

    strip = 256

    def transform(right_table, left_table, finish):
        for start in range(0, size, strip):
            halfway = jnp.dot(
                xbuf[start:start + strip, :], right_table[...], preferred_element_type=F32
            ).astype(BF16)
            ybuf[start:start + strip, :] = halfway[:, :size]
            ybuf[size + start:size + start + strip, :] = halfway[:, size:]
        for start in range(0, size, strip):
            real = jnp.dot(
                left_table[start:start + strip, :], ybuf[...], preferred_element_type=F32
            )
            imag = jnp.dot(
                left_table[size + start:size + start + strip, :], ybuf[...], preferred_element_type=F32
            )
            finish(slice(start, start + strip), real, imag)

    def put(here, real, imag):
        xbuf[here, :size] = real.astype(BF16)
        xbuf[here, size:] = imag.astype(BF16)

    def propagate(field, cut, sign, finish):
        for start in range(0, size, strip):
            here = slice(start, start + strip)
            put(here, *field(here))

        def turn(here, real, imag):
            cosine = trig[cut, 0, here, :]
            sine = trig[cut, 1, here, :] * sign
            put(here, real * cosine - imag * sine, real * sine + imag * cosine)

        transform(fwd, inv, turn)
        transform(inv, fwd, finish)

    def edge_copy(item, cut):
        flip = kind(item, core)
        j = slot_of(item, core)
        return pltpu.make_async_remote_copy(
            terms.at[item, cut], pieces.at[1 - flip, j], edge_ssem.at[item, cut], edge_rsem.at[1 - flip, j],
            device_id={"cuts": cut, "tile": jnp.where(flip == 1, left, right)},
        )

    def final_copy(item, cut):
        return pltpu.make_async_remote_copy(
            terms.at[item, cut], final, edge_ssem.at[item, cut], edge_rsem.at[1, kept - 1],
            device_id={"cuts": cut, "tile": right},
        )

    def is_final(item):
        return (item < 3) & (slot_of(item, core) == kept - 1)

    def send_edge(item, cut):
        @pl.when(has_far(item, core) & is_final(item))
        def _():
            final_copy(item, cut).start()

        @pl.when(has_far(item, core) & jnp.logical_not(is_final(item)))
        def _():
            edge_copy(item, cut).start()

    def part_copy(item):
        return pltpu.make_async_remote_copy(
            terms.at[item, other], pieces.at[kind(item, core), slot_of(item, core)],
            part_ssem.at[item], part_rsem.at[item], device_id=partner,
        )

    def keep_copy(item):
        return pltpu.make_async_copy(
            terms.at[item, core], pieces.at[kind(item, core), slot_of(item, core)], keep_sem.at[item]
        )

    def work(item):
        flip = kind(item, core)
        j = slot_of(item, core)
        row = jnp.bitwise_and(index[flip, j], size - 1)
        column = index[flip, 8 + j]
        live = index[flip, 16 + j] > 0
        to_row = (rows == jnp.bitwise_and(lanes + row, size - 1)).astype(F32).astype(BF16)
        to_lane = (lanes == jnp.bitwise_and(rows + column, size - 1)).astype(F32).astype(BF16)

        def moved(value):
            moving = jnp.dot(value, to_lane, preferred_element_type=F32).astype(BF16)
            return jnp.dot(to_row, moving, preferred_element_type=F32)

        def shifted(value):
            high = value.astype(BF16)
            low = (value - high.astype(F32)).astype(BF16)
            return moved(high) + moved(low)

        for plane in (0, 1):
            psi0[plane] = shifted(probe[plane])
        own_copy(item).wait_recv()
        start = jnp.where(flip == 1, 0, column)
        stop = jnp.where(flip == 1, column, size)
        inside = (lanes >= start) & (lanes < stop)

        @pl.when(has_far(item, core))
        def _():
            for cut in (0, 1):
                pltpu.make_async_remote_copy(
                    send_left.at[0], far.at[j // 2, cut], left_ssem.at[0], far_rsem.at[j // 2, cut],
                    device_id={"cuts": cut, "tile": right},
                ).wait_recv()
                for plane in (0, 1):
                    window[cut, plane] = jnp.where(
                        inside, own[item, cut, plane].astype(F32), far[j // 2, cut, plane].astype(F32)
                    )

        @pl.when(jnp.logical_not(has_far(item, core)))
        def _():
            for cut in (0, 1):
                for plane in (0, 1):
                    window[cut, plane] = jnp.where(inside, own[item, cut, plane].astype(F32), 0.0)

        @pl.when(flip == 1)
        def _():
            level_copy(j // 5).wait_recv()
            measured[...] = level_far[j // 5].astype(F32)

        @pl.when(flip == 0)
        def _():
            measured[...] = intensity[chosen[0, j]]

        measured[...] = shifted(measured[...])

        def enter(wave, cut):
            def field(here):
                real, imag = wave[0, here, :].astype(F32), wave[1, here, :].astype(F32)
                o_real, o_imag = window[cut, 0, here, :], window[cut, 1, here, :]
                return real * o_real - imag * o_imag, real * o_imag + imag * o_real
            return field

        def keep(here, real, imag):
            psi1[0, here, :] = real.astype(BF16)
            psi1[1, here, :] = imag.astype(BF16)

        propagate(enter(psi0, 0), 0, 1.0, keep)

        def residual(here, real, imag):
            real, imag = real.astype(BF16).astype(F32), imag.astype(BF16).astype(F32)
            factor = 2.0 * (real * real + imag * imag - measured[here, :])
            field_[0, here, :] = jnp.where(live, factor * real, 0.0)
            field_[1, here, :] = jnp.where(live, factor * imag, 0.0)

        propagate(enter(psi1, 1), 1, 1.0, residual)

        def stored(here):
            return field_[0, here, :], field_[1, here, :]

        def emit(cut, wave, onward):
            def finish(here, real, imag):
                w_real, w_imag = wave[0, here, :].astype(F32), wave[1, here, :].astype(F32)
                terms[item, cut, 0, here, :] = (w_real * real + w_imag * imag).astype(BF16)
                terms[item, cut, 1, here, :] = (w_real * imag - w_imag * real).astype(BF16)
                if onward:
                    o_real, o_imag = window[cut, 0, here, :], window[cut, 1, here, :]
                    field_[0, here, :] = o_real * real + o_imag * imag
                    field_[1, here, :] = o_real * imag - o_imag * real
            return finish

        propagate(stored, 1, -1.0, emit(1, psi1, True))

        send_edge(item, 1)

        propagate(stored, 0, -1.0, emit(0, psi0, False))

        send_edge(item, 0)

        part_copy(item).start()
        keep_copy(item).start()

    @pl.loop(0, items)
    def _(turn):
        item = lax.rem(turn + 3, items)

        @pl.when(exists(item, core))
        def _():
            work(item)

    phase_copy.wait_send()

    @pl.loop(0, items)
    def _(item):
        @pl.when(exists(item, core))
        def _():
            keep_copy(item).wait()
            part_copy(item).wait_send()

        @pl.when(exists(item, other))
        def _():
            own_copy(item).wait_send()
            part_copy(item).wait_recv()

    strip = 64
    strip_rows = iota((strip, size), 0)
    strip_lanes = iota((strip, size), 1)

    def add_in(base, j):
        row = index[base, j]
        first = lax.shift_right_logical(row, 8)
        begin = jnp.bitwise_and(row, size - 1)
        column = index[base, 8 + j]
        columns = (strip_lanes < column) if base else (strip_lanes >= column)

        @pl.loop(0, canvas.shape[0])
        def _(block):
            below = block - first
            low = jnp.where(below == 0, begin, jnp.where(below == 1, 0, size))
            high = jnp.where(below == 0, size, begin)
            for start in range(0, size, strip):
                mask = columns & (strip_rows >= low - start) & (strip_rows < high - start)
                here = slice(start, start + strip)
                for plane in (0, 1):
                    added = pieces[base, j, plane, here, :].astype(F32)
                    canvas[block, plane, here, :] += jnp.where(mask, added, 0.0)

    def edge_arrives(base, j):
        pltpu.make_async_remote_copy(
            terms.at[0, 0], pieces.at[base, j], edge_ssem.at[0, 0], edge_rsem.at[base, j],
            device_id={"cuts": core, "tile": right},
        ).wait_recv()

    for j in range(kept):
        add_in(0, j)

    @pl.when(has_left)
    def _():
        for j in range(kept, slots):
            add_in(1, j)

    for j in range(kept):

        @pl.when(has_right)
        def _(j=j):
            edge_arrives(0, kept + j)

        add_in(0, kept + j)
        if j < kept - 1:

            @pl.when(has_left)
            def _(j=j):
                edge_arrives(1, j)
                add_in(1, j)

    @pl.loop(0, 3)
    def _(item):
        @pl.when(exists(item, core) & has_far(item, core))
        def _():
            for cut in (0, 1):
                edge_copy(item, cut).wait_send()

    @pl.when(has_right)
    def _():
        index_copy.wait_send()
        level_copy(0).wait_send()

        @pl.when(core == 1)
        def _():
            level_copy(1).wait_send()

        for j in range(kept, slots):
            right_copy(j).wait_send()

    @pl.when(has_left)
    def _():
        for j in range(kept):
            left_copy(j).wait_send()
        final_copy(0, 0).wait_recv()


def deposit_kernel(index_in, canvas, final, out_hbm, summed, sem):
    size = final.shape[-1]
    rows = iota((size, size), 0)
    lanes = iota((size, size), 1)
    first, begin, column = [jnp.max(index_in[k]).astype(jnp.int32) for k in range(3)]

    @pl.loop(0, canvas.shape[0])
    def _(block):
        below = block - first
        touched = (below == 0) | (below == 1)

        @pl.when(jnp.logical_not(touched))
        def _():
            pltpu.make_async_copy(canvas.at[block], out_hbm.at[:, block], sem.at[block]).start()

        @pl.when(touched)
        def _():
            mask = (rows >= jnp.where(below == 0, begin, 0)) & (lanes < column)
            mask = mask & (rows < jnp.where(below == 0, size, begin))
            for plane in (0, 1):
                added = jnp.where(mask, final[plane].astype(F32), 0.0)
                summed[below, plane] = canvas[block, plane] + added
            pltpu.make_async_copy(summed.at[below], out_hbm.at[:, block], sem.at[block]).start()

    @pl.loop(0, canvas.shape[0])
    def _(block):
        pltpu.make_async_copy(canvas.at[block], out_hbm.at[:, block], sem.at[block]).wait()


def on_device(
    object_slices, probe_field, slice_phase, intensity, counts, chosen, row_offset, column_offset
):
    _, _, height, breadth = object_slices.shape
    size = probe_field.shape[-1]
    scan = row_offset.shape[1]
    slots = chosen.shape[1]
    items = slots
    forward, inverse = dft_tables(size)
    anywhere = pl.BlockSpec(memory_space=pl.ANY)
    stay = pl.BlockSpec(memory_space=pltpu.HBM)
    plane = (size, size)
    dma = pltpu.SemaphoreType.DMA
    operands = (
        chosen, row_offset, column_offset,
        object_slices.reshape(2, height // size, size, breadth), probe_field, slice_phase[0],
        intensity[0], jnp.asarray(forward), jnp.asarray(inverse),
    )
    index, canvas, final = pl.pallas_call(
        slot_kernel,
        out_shape=(
            jax.ShapeDtypeStruct((3, 8, 128), F32),
            jax.ShapeDtypeStruct((height // size, 2) + plane, F32),
            jax.ShapeDtypeStruct((2,) + plane, BF16),
        ),
        in_specs=[stay] * 10,
        out_specs=(pl.BlockSpec(memory_space=pltpu.VMEM),) * 2 + (anywhere,),
        scratch_shapes=[
            pltpu.VMEM((2, height // size) + plane, F32),
            pltpu.VMEM((2,) + plane, F32),
            pltpu.VMEM((2,) + plane, F32),
            pltpu.VMEM((2, 2) + plane, F32),
            pltpu.VMEM((scan,) + plane, F32),
            pltpu.VMEM((2 * size, 2 * size), BF16),
            pltpu.VMEM((2 * size, 2 * size), BF16),
            pltpu.VMEM((items, 2, 2) + plane, BF16),
            pltpu.VMEM((items, 2) + plane, BF16),
            pltpu.VMEM((3, 2, 2) + plane, BF16),
            pltpu.VMEM((slots // 2, 2) + plane, BF16),
            pltpu.VMEM((slots // 2, 2) + plane, BF16),
            pltpu.VMEM((2,) + plane, BF16),
            pltpu.VMEM((2,) + plane, BF16),
            pltpu.VMEM(plane, F32),
            pltpu.VMEM((items, 2, 2) + plane, BF16),
            pltpu.VMEM((2, slots, 2) + plane, BF16),
            pltpu.VMEM((2,) + plane, F32),
            pltpu.VMEM((2,) + plane, BF16),
            pltpu.VMEM((2,) + plane, F32),
            pltpu.VMEM((2, 2) + plane, F32),
            pltpu.VMEM((size, 2 * size), BF16),
            pltpu.VMEM((2 * size, size), BF16),
            pltpu.SMEM((2, 32), jnp.int32),
            pltpu.SMEM((1,), jnp.int32),
            pltpu.SMEM((1, slots), jnp.int32),
            pltpu.SMEM((1, scan), jnp.int32),
            pltpu.SMEM((1, scan), jnp.int32),
            dma((10,)),
            dma((2,)),
            dma((2,)),
            dma((2,)),
            dma((2,)),
            dma((items,)),
            dma((items,)),
            dma((slots // 2,)),
            dma((slots // 2,)),
            dma((3, 2)),
            dma((items,)),
            dma((items,)),
            dma((items,)),
            dma((items, 2)),
            dma((2, slots)),
        ],
        compiler_params=pltpu.CompilerParams(
            collective_id=0, has_side_effects=True, vmem_limit_bytes=48 * 1024 * 1024
        ),
        name="slots",
    )(counts, *[pltpu.with_memory_space_constraint(operand, pltpu.HBM) for operand in operands])
    gradient = pl.pallas_call(
        deposit_kernel,
        in_specs=[pl.BlockSpec(memory_space=pltpu.VMEM)] * 3,
        out_specs=anywhere,
        out_shape=jax.ShapeDtypeStruct((2, height // size, size, breadth), F32),
        scratch_shapes=[
            pltpu.VMEM((2, 2) + plane, F32),
            dma((height // size,)),
        ],
        compiler_params=pltpu.CompilerParams(vmem_limit_bytes=16 * 1024 * 1024),
        name="deposit",
    )(index, canvas, final)
    return gradient.reshape(1, 2, height, breadth)


def solution(mesh):
    return jax.shard_map(
        on_device,
        mesh=mesh,
        in_specs=(
            P("cuts", None, None, "tile"),
            P(),
            P("cuts", None, None),
            P("tile", None, None, None),
            P("tile"),
            P("tile", None),
            P("tile", None),
            P("tile", None),
        ),
        out_specs=P("cuts", None, None, "tile"),
        check_vma=False,
    )
```

```python
import jax
import jax.numpy as jnp
import numpy as np
from jax import lax
from jax.experimental import pallas as pl
from jax.experimental.pallas import tpu as pltpu
from jax.sharding import PartitionSpec as P

BF16 = jnp.bfloat16
F32 = jnp.float32


def dft_tables(length):
    index = np.arange(length, dtype=np.int32)
    product = index[:, None] * index[None, :] % length
    angle = product.astype(np.float32) * np.float32(2.0 * np.pi / length)
    scale = np.float32(length ** (-0.5))
    cosine = np.cos(angle) * scale
    sine = np.sin(angle) * scale
    forward = np.block([[cosine, -sine], [sine, cosine]])
    inverse = np.block([[cosine, sine], [-sine, cosine]])
    return forward.astype(BF16), inverse.astype(BF16)


def iota(shape, axis):
    return lax.broadcasted_iota(jnp.int32, shape, axis)


def slot_of(item, cut):
    return lax.rem(3 * cut + 4 * item, 6)


def slot_kernel(
    counts_hbm, chosen_hbm, row_hbm, column_hbm,
    obj_hbm, probe_hbm, phase_hbm, intensity_hbm, fwd_hbm, inv_hbm,
    index_out, canvas, final,
    obj, probe, phase, trig, intensity, fwd, inv,
    own, own_send, far, send_left, send_right, level_send, level_far, measured,
    terms, pieces, psi0, psi1, field_, window, xbuf, ybuf,
    index, counts, chosen, row_offset, column_offset,
    in_sem, index_sem, phase_sem, level_ssem, level_rsem, own_ssem, own_rsem, left_ssem, right_ssem, far_rsem,
    keep_sem, part_ssem, part_rsem, edge_ssem, edge_rsem,
):
    slots = chosen.shape[1]
    kept = slots // 2
    size = probe.shape[-1]
    items = terms.shape[0]
    last_block = obj.shape[1] - 1
    core = lax.axis_index("cuts")
    tile = lax.axis_index("tile")
    tiles = lax.axis_size("tile")
    other = 1 - core
    right = lax.rem(tile + 1, tiles)
    left = lax.rem(tile + tiles - 1, tiles)
    has_left = tile > 0
    has_right = tile < tiles - 1
    partner = {"cuts": other, "tile": tile}

    def copy_in(source, target, number):
        return pltpu.make_async_copy(source, target, in_sem.at[number])

    scalars = [
        copy_in(counts_hbm, counts, 0),
        copy_in(chosen_hbm, chosen, 1),
        copy_in(row_hbm, row_offset, 2),
        copy_in(column_hbm, column_offset, 3),
    ]
    load_obj = copy_in(obj_hbm, obj, 4)
    load_phase = copy_in(phase_hbm, phase.at[core], 5)
    load_intensity = copy_in(intensity_hbm, intensity, 6)
    rest = [copy_in(probe_hbm, probe, 7), copy_in(fwd_hbm, fwd, 8), copy_in(inv_hbm, inv, 9)]
    @pl.when(tile == 0)
    def _():
        for k in range(32):
            index[1, k] = 0

    barrier = pltpu.get_barrier_semaphore()
    pl.semaphore_signal(barrier, inc=1, device_id=partner)
    for there, reached in ((left, has_left), (right, has_right)):

        @pl.when(reached)
        def _(there=there):
            for cut in (0, 1):
                pl.semaphore_signal(barrier, inc=1, device_id={"cuts": cut, "tile": there})

    for load in scalars + [load_obj, load_phase, load_intensity] + rest:
        load.start()

    for k in range(32):
        index[0, k] = 0
    for load in scalars:
        load.wait()
    for j in range(slots):
        q = chosen[0, j]
        index[0, j] = row_offset[0, q]
        index[0, 8 + j] = column_offset[0, q]
        index[0, 16 + j] = (j < counts[0]).astype(jnp.int32)

    rows = iota((size, size), 0)
    lanes = iota((size, size), 1)

    def fold(row, plane):
        block = lax.shift_right_logical(row, 8)
        after = jnp.minimum(block + 1, last_block)
        here = obj[plane, block]
        below = obj[plane, after]
        return jnp.where(rows >= jnp.bitwise_and(row, size - 1), here, below).astype(BF16)

    index_copy = pltpu.make_async_remote_copy(
        index.at[0], index.at[1], index_sem.at[0], index_sem.at[1],
        device_id={"cuts": core, "tile": right},
    )
    phase_copy = pltpu.make_async_remote_copy(
        phase.at[core], phase.at[core], phase_sem.at[0], phase_sem.at[1], device_id=partner
    )
    def level_copy(n):
        return pltpu.make_async_remote_copy(
            level_send.at[n], level_far.at[n], level_ssem.at[n], level_rsem.at[n],
            device_id={"cuts": core, "tile": right},
        )

    def right_copy(j):
        return pltpu.make_async_remote_copy(
            send_right.at[j - kept], far.at[j // 2, core],
            right_ssem.at[j - kept], far_rsem.at[j // 2, core],
            device_id={"cuts": j % 2, "tile": right},
        )

    def left_copy(j):
        return pltpu.make_async_remote_copy(
            send_left.at[j], far.at[j // 2, core], left_ssem.at[j], far_rsem.at[j // 2, core],
            device_id={"cuts": j % 2, "tile": left},
        )

    def own_copy(item):
        return pltpu.make_async_remote_copy(
            own_send.at[item], own.at[item, core], own_ssem.at[item], own_rsem.at[item],
            device_id=partner,
        )

    def kind(item, cut):
        return ((item < 3) & (slot_of(item, cut) >= kept)).astype(jnp.int32)

    def exists(item, cut):
        away = slot_of(item, cut) >= kept
        usual = (item < 3) & (jnp.logical_not(away) | has_left)
        return usual | ((item >= 3) & away & jnp.logical_not(has_right))

    def has_far(item, cut):
        return jnp.where(kind(item, cut) == 1, has_left, has_right)

    def near_windows(first, last, flip):
        @pl.loop(first, last)
        def _(item):
            @pl.when(exists(item, other) & (kind(item, other) == flip))
            def _():
                row = index[flip, slot_of(item, other)]
                for plane in (0, 1):
                    own_send[item, plane] = fold(row, plane)
                own_copy(item).start()

            @pl.when(exists(item, core) & (kind(item, core) == flip))
            def _():
                row = index[flip, slot_of(item, core)]
                for plane in (0, 1):
                    own[item, core, plane] = fold(row, plane)

    peers = 1 + 2 * has_left.astype(jnp.int32) + 2 * has_right.astype(jnp.int32)
    load_obj.wait()
    for plane in (0, 1):
        send_right[0, plane] = fold(index[0, kept], plane)
    pl.semaphore_wait(barrier, peers)

    @pl.when(has_right)
    def _():
        index_copy.start()

    load_intensity.wait()
    level_send[0] = intensity[chosen[0, 4 - core]].astype(BF16)
    level_send[1] = intensity[chosen[0, 5]].astype(BF16)

    @pl.when(has_right)
    def _():
        @pl.when(core == 1)
        def _():
            level_copy(0).start()

        right_copy(kept).start()

        @pl.when(core == 0)
        def _():
            level_copy(0).start()

        for plane in (0, 1):
            send_right[1, plane] = fold(index[0, kept + 1], plane)
        right_copy(kept + 1).start()

        @pl.when(core == 1)
        def _():
            level_copy(1).start()

        for plane in (0, 1):
            send_right[2, plane] = fold(index[0, kept + 2], plane)
        right_copy(kept + 2).start()

    load_phase.wait()
    phase_copy.start()
    near_windows(0, 3, 0)

    @pl.when(has_left)
    def _():
        index_copy.wait_recv()
        for j in range(kept):
            for plane in (0, 1):
                send_left[j, plane] = fold(index[1, j], plane)
            left_copy(j).start()

    @pl.when(has_left)
    def _():
        near_windows(0, 3, 1)

    @pl.when(jnp.logical_not(has_right))
    def _():
        near_windows(3, items, 0)

    last_live = (index[1, 16 + kept - 1] > 0) & has_left
    placed = (
        jnp.where(last_live, lax.shift_right_logical(index[1, kept - 1], 8), -9),
        jnp.bitwise_and(index[1, kept - 1], size - 1),
        index[1, 8 + kept - 1],
    )
    for k in range(3):
        index_out[k] = jnp.full(index_out.shape[1:], placed[k], jnp.int32).astype(F32)

    @pl.loop(0, canvas.shape[0])
    def _(block):
        canvas[block] = jnp.zeros(canvas.shape[1:], F32)

    phase_copy.wait_recv()

    @pl.loop(0, 2 * size // 32)
    def _(k):
        cut = k // (size // 32)
        start = pl.multiple_of(lax.rem(k, size // 32) * 32, 32)
        angle = phase[cut, pl.ds(start, 32), :]
        trig[cut, 0, pl.ds(start, 32), :] = jnp.cos(angle)
        trig[cut, 1, pl.ds(start, 32), :] = jnp.sin(angle)

    for load in rest:
        load.wait()

    strip = 256

    def transform(right_table, left_table, finish):
        for start in range(0, size, strip):
            halfway = jnp.dot(
                xbuf[start:start + strip, :], right_table[...], preferred_element_type=F32
            ).astype(BF16)
            ybuf[start:start + strip, :] = halfway[:, :size]
            ybuf[size + start:size + start + strip, :] = halfway[:, size:]
        for start in range(0, size, strip):
            real = jnp.dot(
                left_table[start:start + strip, :], ybuf[...], preferred_element_type=F32
            )
            imag = jnp.dot(
                left_table[size + start:size + start + strip, :], ybuf[...], preferred_element_type=F32
            )
            finish(slice(start, start + strip), real, imag)

    def put(here, real, imag):
        xbuf[here, :size] = real.astype(BF16)
        xbuf[here, size:] = imag.astype(BF16)

    def propagate(field, cut, sign, finish):
        for start in range(0, size, strip):
            here = slice(start, start + strip)
            put(here, *field(here))

        def turn(here, real, imag):
            cosine = trig[cut, 0, here, :]
            sine = trig[cut, 1, here, :] * sign
            put(here, real * cosine - imag * sine, real * sine + imag * cosine)

        transform(fwd, inv, turn)
        transform(inv, fwd, finish)

    def edge_copy(item, cut):
        flip = kind(item, core)
        j = slot_of(item, core)
        return pltpu.make_async_remote_copy(
            terms.at[item, cut], pieces.at[1 - flip, j], edge_ssem.at[item, cut], edge_rsem.at[1 - flip, j],
            device_id={"cuts": cut, "tile": jnp.where(flip == 1, left, right)},
        )

    def final_copy(item, cut):
        return pltpu.make_async_remote_copy(
            terms.at[item, cut], final, edge_ssem.at[item, cut], edge_rsem.at[1, kept - 1],
            device_id={"cuts": cut, "tile": right},
        )

    def is_final(item):
        return (item < 3) & (slot_of(item, core) == kept - 1)

    def send_edge(item, cut):
        @pl.when(has_far(item, core) & is_final(item))
        def _():
            final_copy(item, cut).start()

        @pl.when(has_far(item, core) & jnp.logical_not(is_final(item)))
        def _():
            edge_copy(item, cut).start()

    def part_copy(item):
        return pltpu.make_async_remote_copy(
            terms.at[item, other], pieces.at[kind(item, core), slot_of(item, core)],
            part_ssem.at[item], part_rsem.at[item], device_id=partner,
        )

    def keep_copy(item):
        return pltpu.make_async_copy(
            terms.at[item, core], pieces.at[kind(item, core), slot_of(item, core)], keep_sem.at[item]
        )

    def work(item):
        flip = kind(item, core)
        j = slot_of(item, core)
        row = jnp.bitwise_and(index[flip, j], size - 1)
        column = index[flip, 8 + j]
        live = index[flip, 16 + j] > 0
        to_row = (rows == jnp.bitwise_and(lanes + row, size - 1)).astype(F32).astype(BF16)
        to_lane = (lanes == jnp.bitwise_and(rows + column, size - 1)).astype(F32).astype(BF16)

        def moved(value):
            moving = jnp.dot(value, to_lane, preferred_element_type=F32).astype(BF16)
            return jnp.dot(to_row, moving, preferred_element_type=F32)

        def shifted(value):
            high = value.astype(BF16)
            low = (value - high.astype(F32)).astype(BF16)
            return moved(high) + moved(low)

        for plane in (0, 1):
            psi0[plane] = shifted(probe[plane])
        own_copy(item).wait_recv()
        start = jnp.where(flip == 1, 0, column)
        stop = jnp.where(flip == 1, column, size)
        inside = (lanes >= start) & (lanes < stop)

        @pl.when(has_far(item, core))
        def _():
            for cut in (0, 1):
                pltpu.make_async_remote_copy(
                    send_left.at[0], far.at[j // 2, cut], left_ssem.at[0], far_rsem.at[j // 2, cut],
                    device_id={"cuts": cut, "tile": right},
                ).wait_recv()
                for plane in (0, 1):
                    window[cut, plane] = jnp.where(
                        inside, own[item, cut, plane].astype(F32), far[j // 2, cut, plane].astype(F32)
                    )

        @pl.when(jnp.logical_not(has_far(item, core)))
        def _():
            for cut in (0, 1):
                for plane in (0, 1):
                    window[cut, plane] = jnp.where(inside, own[item, cut, plane].astype(F32), 0.0)

        @pl.when(flip == 1)
        def _():
            level_copy(j // 5).wait_recv()
            measured[...] = level_far[j // 5].astype(F32)

        @pl.when(flip == 0)
        def _():
            measured[...] = intensity[chosen[0, j]]

        measured[...] = shifted(measured[...])

        def enter(wave, cut):
            def field(here):
                real, imag = wave[0, here, :].astype(F32), wave[1, here, :].astype(F32)
                o_real, o_imag = window[cut, 0, here, :], window[cut, 1, here, :]
                return real * o_real - imag * o_imag, real * o_imag + imag * o_real
            return field

        def keep(here, real, imag):
            psi1[0, here, :] = real.astype(BF16)
            psi1[1, here, :] = imag.astype(BF16)

        propagate(enter(psi0, 0), 0, 1.0, keep)

        def residual(here, real, imag):
            real, imag = real.astype(BF16).astype(F32), imag.astype(BF16).astype(F32)
            factor = 2.0 * (real * real + imag * imag - measured[here, :])
            field_[0, here, :] = jnp.where(live, factor * real, 0.0)
            field_[1, here, :] = jnp.where(live, factor * imag, 0.0)

        propagate(enter(psi1, 1), 1, 1.0, residual)

        def stored(here):
            return field_[0, here, :], field_[1, here, :]

        def emit(cut, wave, onward):
            def finish(here, real, imag):
                w_real, w_imag = wave[0, here, :].astype(F32), wave[1, here, :].astype(F32)
                terms[item, cut, 0, here, :] = (w_real * real + w_imag * imag).astype(BF16)
                terms[item, cut, 1, here, :] = (w_real * imag - w_imag * real).astype(BF16)
                if onward:
                    o_real, o_imag = window[cut, 0, here, :], window[cut, 1, here, :]
                    field_[0, here, :] = o_real * real + o_imag * imag
                    field_[1, here, :] = o_real * imag - o_imag * real
            return finish

        propagate(stored, 1, -1.0, emit(1, psi1, True))

        send_edge(item, 1)

        propagate(stored, 0, -1.0, emit(0, psi0, False))

        send_edge(item, 0)

        part_copy(item).start()
        keep_copy(item).start()

    @pl.loop(0, items)
    def _(turn):
        item = lax.rem(turn + 3, items)

        @pl.when(exists(item, core))
        def _():
            work(item)

    phase_copy.wait_send()

    @pl.loop(0, items)
    def _(item):
        @pl.when(exists(item, core))
        def _():
            keep_copy(item).wait()
            part_copy(item).wait_send()

        @pl.when(exists(item, other))
        def _():
            own_copy(item).wait_send()
            part_copy(item).wait_recv()

    strip = 64
    strip_rows = iota((strip, size), 0)
    strip_lanes = iota((strip, size), 1)

    def add_in(base, j):
        row = index[base, j]
        first = lax.shift_right_logical(row, 8)
        begin = jnp.bitwise_and(row, size - 1)
        column = index[base, 8 + j]
        columns = (strip_lanes < column) if base else (strip_lanes >= column)

        @pl.loop(0, canvas.shape[0])
        def _(block):
            below = block - first
            low = jnp.where(below == 0, begin, jnp.where(below == 1, 0, size))
            high = jnp.where(below == 0, size, begin)
            for start in range(0, size, strip):
                mask = columns & (strip_rows >= low - start) & (strip_rows < high - start)
                here = slice(start, start + strip)
                for plane in (0, 1):
                    added = pieces[base, j, plane, here, :].astype(F32)
                    canvas[block, plane, here, :] += jnp.where(mask, added, 0.0)

    def edge_arrives(base, j):
        pltpu.make_async_remote_copy(
            terms.at[0, 0], pieces.at[base, j], edge_ssem.at[0, 0], edge_rsem.at[base, j],
            device_id={"cuts": core, "tile": right},
        ).wait_recv()

    for j in range(kept):
        add_in(0, j)

    @pl.when(has_left)
    def _():
        for j in range(kept, slots):
            add_in(1, j)

    for j in range(kept):

        @pl.when(has_right)
        def _(j=j):
            edge_arrives(0, kept + j)

        add_in(0, kept + j)
        if j < kept - 1:

            @pl.when(has_left)
            def _(j=j):
                edge_arrives(1, j)
                add_in(1, j)

    @pl.loop(0, 3)
    def _(item):
        @pl.when(exists(item, core) & has_far(item, core))
        def _():
            for cut in (0, 1):
                edge_copy(item, cut).wait_send()

    @pl.when(has_right)
    def _():
        index_copy.wait_send()
        level_copy(0).wait_send()

        @pl.when(core == 1)
        def _():
            level_copy(1).wait_send()

        for j in range(kept, slots):
            right_copy(j).wait_send()

    @pl.when(has_left)
    def _():
        for j in range(kept):
            left_copy(j).wait_send()
        final_copy(0, 0).wait_recv()


def deposit_kernel(index_in, canvas, final, out_hbm, summed, sem):
    size = final.shape[-1]
    rows = iota((size, size), 0)
    lanes = iota((size, size), 1)
    first, begin, column = [jnp.max(index_in[k]).astype(jnp.int32) for k in range(3)]

    @pl.loop(0, canvas.shape[0])
    def _(block):
        below = block - first
        touched = (below == 0) | (below == 1)

        @pl.when(jnp.logical_not(touched))
        def _():
            pltpu.make_async_copy(canvas.at[block], out_hbm.at[:, block], sem.at[block]).start()

        @pl.when(touched)
        def _():
            mask = (rows >= jnp.where(below == 0, begin, 0)) & (lanes < column)
            mask = mask & (rows < jnp.where(below == 0, size, begin))
            for plane in (0, 1):
                added = jnp.where(mask, final[plane].astype(F32), 0.0)
                summed[below, plane] = canvas[block, plane] + added
            pltpu.make_async_copy(summed.at[below], out_hbm.at[:, block], sem.at[block]).start()

    @pl.loop(0, canvas.shape[0])
    def _(block):
        pltpu.make_async_copy(canvas.at[block], out_hbm.at[:, block], sem.at[block]).wait()


def on_device(
    object_slices, probe_field, slice_phase, intensity, counts, chosen, row_offset, column_offset
):
    _, _, height, breadth = object_slices.shape
    size = probe_field.shape[-1]
    scan = row_offset.shape[1]
    slots = chosen.shape[1]
    items = slots
    forward, inverse = dft_tables(size)
    anywhere = pl.BlockSpec(memory_space=pl.ANY)
    stay = pl.BlockSpec(memory_space=pltpu.HBM)
    plane = (size, size)
    dma = pltpu.SemaphoreType.DMA
    operands = (
        chosen, row_offset, column_offset,
        object_slices.reshape(2, height // size, size, breadth), probe_field, slice_phase[0],
        intensity[0], jnp.asarray(forward), jnp.asarray(inverse),
    )
    index, canvas, final = pl.pallas_call(
        slot_kernel,
        out_shape=(
            jax.ShapeDtypeStruct((3, 8, 128), F32),
            jax.ShapeDtypeStruct((height // size, 2) + plane, F32),
            jax.ShapeDtypeStruct((2,) + plane, BF16),
        ),
        in_specs=[stay] * 10,
        out_specs=(pl.BlockSpec(memory_space=pltpu.VMEM),) * 2 + (anywhere,),
        scratch_shapes=[
            pltpu.VMEM((2, height // size) + plane, F32),
            pltpu.VMEM((2,) + plane, F32),
            pltpu.VMEM((2,) + plane, F32),
            pltpu.VMEM((2, 2) + plane, F32),
            pltpu.VMEM((scan,) + plane, F32),
            pltpu.VMEM((2 * size, 2 * size), BF16),
            pltpu.VMEM((2 * size, 2 * size), BF16),
            pltpu.VMEM((items, 2, 2) + plane, BF16),
            pltpu.VMEM((items, 2) + plane, BF16),
            pltpu.VMEM((3, 2, 2) + plane, BF16),
            pltpu.VMEM((slots // 2, 2) + plane, BF16),
            pltpu.VMEM((slots // 2, 2) + plane, BF16),
            pltpu.VMEM((2,) + plane, BF16),
            pltpu.VMEM((2,) + plane, BF16),
            pltpu.VMEM(plane, F32),
            pltpu.VMEM((items, 2, 2) + plane, BF16),
            pltpu.VMEM((2, slots, 2) + plane, BF16),
            pltpu.VMEM((2,) + plane, F32),
            pltpu.VMEM((2,) + plane, BF16),
            pltpu.VMEM((2,) + plane, F32),
            pltpu.VMEM((2, 2) + plane, F32),
            pltpu.VMEM((size, 2 * size), BF16),
            pltpu.VMEM((2 * size, size), BF16),
            pltpu.SMEM((2, 32), jnp.int32),
            pltpu.SMEM((1,), jnp.int32),
            pltpu.SMEM((1, slots), jnp.int32),
            pltpu.SMEM((1, scan), jnp.int32),
            pltpu.SMEM((1, scan), jnp.int32),
            dma((10,)),
            dma((2,)),
            dma((2,)),
            dma((2,)),
            dma((2,)),
            dma((items,)),
            dma((items,)),
            dma((slots // 2,)),
            dma((slots // 2,)),
            dma((3, 2)),
            dma((items,)),
            dma((items,)),
            dma((items,)),
            dma((items, 2)),
            dma((2, slots)),
        ],
        compiler_params=pltpu.CompilerParams(
            collective_id=0, has_side_effects=True, vmem_limit_bytes=48 * 1024 * 1024
        ),
        name="slots",
    )(counts, *[pltpu.with_memory_space_constraint(operand, pltpu.HBM) for operand in operands])
    gradient = pl.pallas_call(
        deposit_kernel,
        in_specs=[pl.BlockSpec(memory_space=pltpu.VMEM)] * 3,
        out_specs=anywhere,
        out_shape=jax.ShapeDtypeStruct((2, height // size, size, breadth), F32),
        scratch_shapes=[
            pltpu.VMEM((2, 2) + plane, F32),
            dma((height // size,)),
        ],
        compiler_params=pltpu.CompilerParams(vmem_limit_bytes=16 * 1024 * 1024),
        name="deposit",
    )(index, canvas, final)
    return gradient.reshape(1, 2, height, breadth)


def solution(mesh):
    return jax.shard_map(
        on_device,
        mesh=mesh,
        in_specs=(
            P("cuts", None, None, "tile"),
            P(),
            P("cuts", None, None),
            P("tile", None, None, None),
            P("tile"),
            P("tile", None),
            P("tile", None),
            P("tile", None),
        ),
        out_specs=P("cuts", None, None, "tile"),
        check_vma=False,
    )
```
